256 devices in a mesh: dp: 8 (over x, core), tensor: 32 (over y, z).
Axes of the slice: x: 4, y: 4, z: 8, core: 2. Of those that a mesh axis runs over, the one named last changes fastest.
Arguments:
- tokens: bfloat16 [16384, 2048], P(('dp', 'tensor')), may hold values from -6 to 6
- attn_gain: float32 [2048], replicated, may hold values from 0.25 to 1.75
- ffn_gain: float32 [2048], replicated, may hold values from 0.25 to 1.75
- w_attn: bfloat16 [4, 2048, 1024], P(None, None, 'tensor')
- kv_pool: bfloat16 [768, 8, 128, 256], P(('dp', 'tensor'))
- page_table: int32 [8, 72], P('dp'), may hold values from 0 to 95, as said below
- cache_len: int32 [8], P('dp'), may hold values from 2304 to 9216
- routes: int32 [16384, 4], P(('dp', 'tensor')), may hold values from 0 to 63, all different within a row; in each aligned block of 64 rows (0 to 63, 64 to 127, ...) at most 5 rows name the same one
- route_gain: float32 [16384, 4], P(('dp', 'tensor')), may hold values from 0.05 to 0.3
- w_gate_up: bfloat16 [256, 2048, 512], P(('dp', 'tensor')), may hold values from -0.125 to 0.125
- w_down: bfloat16 [256, 256, 2048], P(('dp', 'tensor')), may hold values from -0.1875 to 0.1875
Outputs:
- layer_out: bfloat16 [16384, 2048], P(('dp', 'tensor'))
The draws below stay inside these ranges and needn't reach their ends.
Inputs may be any that keep to these rules, and one draw needn't show every extreme that they name: `page_table`: each row lists 72 different slots; an entry of value v names slot v % 3 of the device v // 3 along tensor in the request's pool. `routes`: among the 64 tokens of one device no expert is named more than 5 times, and in every draw some expert is named exactly 5 times by one device's tokens. A row names 4 different experts.
All inputs are finite; a program needn't handle non-finite values.
Results may differ from the reference program's by a relative error of at most 0.014.
Values may be sent and summed in bfloat16 or wider, within the bound.
A program may use at most 128 MiB of HBM per device.

```python
import math
import jax
import jax.numpy as jnp
import numpy as np
from jax import lax

D = 2048
HEADS = 8
HD = 128
EXPERTS = 64
FF = 1024
TOP = 4
PAGE = 128
TOK_DEV = 64
CAP = 5
SPAN = 2048
REQS = 8
TOKENS = 16384
GROUP_SLOTS = 96
POOL = 768
MAXP = 72
MAXLEN = 9216
HIDDEN_PIECES = 4
PIECE_HIDDEN = 256
EXP_DP = 8
PIECES = 256
N_DP = 8


def draw_w_attn(key, part):
    values = jax.random.normal(key, (4, D, HEADS * HD), jnp.float32) / math.sqrt(D)
    return values.astype(jnp.bfloat16)


def draw_kv_pool(key, part):
    values = jax.random.normal(key, (POOL, HEADS, PAGE, 2 * HD), jnp.float32)
    return values.astype(jnp.bfloat16)


def draw_page_table(key, part):
    keys = jax.random.split(key, REQS)

    def one_row(row_key):
        return jax.random.permutation(row_key, GROUP_SLOTS)[:MAXP].astype(jnp.int32)
    return jax.vmap(one_row)(keys)


def touch_ends(values, rng, least, high):
    extent = values.shape
    index_at = [jax.random.randint(jax.random.fold_in(rng, axis), (), 0, extent[axis]) for axis in range(len(extent))]
    values = values.at[tuple(index_at)].set(least)
    longest = extent.index(max(extent))
    index_at[longest] = (index_at[longest] + 1) % extent[longest]
    return values.at[tuple(index_at)].set(high)


def block_levels(rng, extent, cuts, smallest, high):
    def one(dim, blocks):
        heights = jax.random.uniform(jax.random.fold_in(jax.random.fold_in(rng, 6), dim), (blocks,), jnp.float32, smallest / len(cuts), high / len(cuts))
        return jnp.repeat(jnp.exp(heights), extent[dim] // blocks).reshape((-1,) + (1,) * (len(extent) - dim - 1))

    loudness = one(*cuts[0])
    for cut in cuts[1:]:
        loudness = loudness * one(*cut)
    return loudness


def shared_out(key, own, number, rows, number_of, top, limit, slope):
    ranking = jax.random.permutation(key, number_of)
    crowded, ordinary = portions_of(number_of, rows * top, limit, slope, True), portions_of(number_of, rows * top, limit, slope, False)
    places = jnp.arange(number_of)

    def named(tallies, offset_by):
        used = int((tallies > 0).sum())
        fixed = max(1, used // 4)
        shifted = fixed + (places - fixed + offset_by * (used - fixed)) % max(1, number_of - fixed)
        return jnp.zeros((number_of,), jnp.int32).at[ranking[jnp.where(places < fixed, places, shifted)]].set(jnp.asarray(tallies, jnp.int32))

    tallies = jnp.where(number % 4 == 0, named(crowded, number // 4), named(ordinary, number - number // 4 - 1))
    mixed = jax.random.permutation(jax.random.fold_in(own, 3), number_of)
    source_of, taker = mixed[0:number_of // 2 * 2:2], mixed[1:number_of // 2 * 2:2]
    room = jnp.minimum(tallies[source_of] - 1, limit - tallies[taker]) // 2
    room = jnp.where((source_of == ranking[0]) | (taker == ranking[0]) | (tallies[taker] == 0), 0, jnp.maximum(room, 0))
    shifted = jax.random.randint(jax.random.fold_in(own, 4), (number_of // 2,), 0, 1 << 20) % (room + 1)
    tallies = tallies.at[source_of].add(-shifted).at[taker].add(shifted)
    members = jnp.searchsorted(jnp.cumsum(tallies), jnp.arange(rows * top), side="right").astype(jnp.int32)
    table = members.reshape(top, rows).T
    table = table[jax.random.permutation(jax.random.fold_in(own, 1), rows)]
    offset_by = jax.random.randint(jax.random.fold_in(own, 2), (rows, 1), 0, top)
    return jnp.take_along_axis(table, (jnp.arange(top)[None, :] + offset_by) % top, axis=1)


def portions_of(amount, total, reach, lean, full):
    weights = [(1 << 20) // math.isqrt(grade ** lean) + 1 for grade in range(1, amount + 1)]
    largest = reach if full else min(reach, max(-(-total // amount), total * weights[0] // sum(weights)))
    least = 1 if total - largest >= amount - 1 else 0
    given, surplus = [largest] + [least] * (amount - 1), total - largest - least * (amount - 1)
    while surplus > 0:
        movable = [i for i in range(1, amount) if given[i] < largest] or [i for i in range(1, amount) if given[i] < reach]
        whole, budget = sum([weights[i] for i in movable]), surplus
        for i in movable:
            extra = min(reach - given[i], max(1, budget * weights[i] // whole), surplus)
            given[i] = given[i] + extra
            surplus = surplus - extra
    return np.array(given)


def scatter_about(stream_key, dims, width, reach, shards=(), kind=jnp.bfloat16):
    array = jax.random.normal(stream_key, dims, jnp.float32) * width
    if len(shards) > 0:
        array = block_levels(stream_key, dims, shards, -0.22, 0.18) * array
    return jnp.clip(array, min=-reach, max=reach).astype(kind)


def setup_inputs(seed: int = 0) -> dict:
    arg_keys = jax.random.split(jax.random.key(seed), 12)
    tokens = scatter_about(arg_keys[0], (TOKENS, D), 1.0, 6.0, ((0, 256),))
    attn_gain = jnp.clip(1.0 + 0.15 * jax.random.normal(arg_keys[1], (D,), jnp.float32), 0.25, 1.75)
    ffn_gain = jnp.clip(1.0 + 0.15 * jax.random.normal(arg_keys[2], (D,), jnp.float32), 0.25, 1.75)
    w_attn = draw_w_attn(jax.random.fold_in(arg_keys[11], 71), 0)
    kv_pool = draw_kv_pool(jax.random.fold_in(arg_keys[11], 71), 0)
    page_table = draw_page_table(jax.random.fold_in(arg_keys[11], 71), 0)
    cache_len = touch_ends(jax.random.randint(arg_keys[6], (REQS,), MAXLEN // 4, MAXLEN + 1), jax.random.fold_in(arg_keys[6], 1), MAXLEN // 4, MAXLEN).astype(jnp.int32)
    routes_keys = jax.random.split(jax.random.fold_in(arg_keys[7], 1), TOKENS // TOK_DEV)
    routes_turns = jax.random.permutation(jax.random.fold_in(arg_keys[7], 3), TOKENS // TOK_DEV)
    routes = jax.vmap(lambda own, number: shared_out(jax.random.fold_in(arg_keys[7], 2), own, number, TOK_DEV, EXPERTS, TOP, CAP, 2))(routes_keys, routes_turns).reshape((TOKENS, TOP))
    route_gain = jnp.clip(0.05 + 0.25 * jax.random.uniform(arg_keys[8], (TOKENS, TOP), jnp.float32) ** block_levels(arg_keys[8], (TOKENS, TOP), ((0, 256),), -0.2, 0.2), 0.05, 0.3)
    w_gate_up = scatter_about(arg_keys[9], (PIECES, D, 2 * PIECE_HIDDEN), D ** -0.5, 0.125, ((0, 256),))
    w_down = scatter_about(arg_keys[10], (PIECES, PIECE_HIDDEN, D), FF ** -0.5, 0.1875, ((0, 256),))
    return {"tokens": tokens, "attn_gain": attn_gain, "ffn_gain": ffn_gain, "w_attn": w_attn, "kv_pool": kv_pool, "page_table": page_table, "cache_len": cache_len, "routes": routes, "route_gain": route_gain, "w_gate_up": w_gate_up, "w_down": w_down}


rope_base = 50000.0
norm_eps = 1e-06
very_low = -1e+30

def rms_scale(rows, gain):
    values = rows.astype(jnp.float32)
    power = lax.optimization_barrier(jnp.mean(values * values, axis=-1, keepdims=True))
    return (values * lax.rsqrt(power + norm_eps) * gain.astype(jnp.float32)).astype(jnp.bfloat16)

def rotate(values, positions):
    half = values.shape[-1] // 2
    freq = rope_base ** (-(jnp.arange(half, dtype=jnp.float32) * 2.0) / values.shape[-1])
    angle = positions.astype(jnp.float32)[:, None] * freq[None, :]
    cosine = jnp.cos(angle)
    sine = jnp.sin(angle)
    first = values[:, :half]
    second = values[:, half:]
    return jnp.concatenate([first * cosine - second * sine, second * cosine + first * sine], axis=1)

def reference(tokens, attn_gain, ffn_gain, w_attn, kv_pool, page_table, cache_len, routes, route_gain, w_gate_up, w_down):
    normed = rms_scale(tokens, attn_gain)
    scale = 1.0 / math.sqrt(HD)

    def one_request(request):
        rows = lax.dynamic_slice_in_dim(normed, request * SPAN, SPAN, 0)
        length = cache_len[request]
        positions = length + jnp.arange(SPAN, dtype=jnp.int32)
        pool = lax.dynamic_slice_in_dim(kv_pool, (request * GROUP_SLOTS).astype(jnp.int32), GROUP_SLOTS, 0)
        pages = jnp.take(pool, page_table[request], axis=0)
        live = jnp.concatenate([jnp.arange(MAXP * PAGE, dtype=jnp.int32) < length, jnp.ones((SPAN,), dtype=bool)])

        def one_head(head):
            weights = lax.dynamic_slice_in_dim(w_attn, (head * HD).astype(jnp.int32), HD, 2)
            query = rotate(jnp.dot(rows, weights[0], preferred_element_type=jnp.float32), positions).astype(jnp.bfloat16)
            key_new = rotate(jnp.dot(rows, weights[1], preferred_element_type=jnp.float32), positions).astype(jnp.bfloat16)
            value_new = jnp.dot(rows, weights[2], preferred_element_type=jnp.float32).astype(jnp.bfloat16)
            cached = lax.dynamic_index_in_dim(pages, head, 1, keepdims=False).reshape(MAXP * PAGE, 2 * HD)
            keys = jnp.concatenate([cached[:, :HD], key_new], axis=0)
            values = jnp.concatenate([cached[:, HD:], value_new], axis=0)
            scores = lax.dot_general(query, keys, (((1,), (1,)), ((), ())), preferred_element_type=jnp.float32) * scale
            scores = jnp.where(live[None, :], scores, very_low)
            top = lax.optimization_barrier(jnp.max(scores, axis=1))
            expo = jnp.exp(scores - top[:, None])
            total = lax.optimization_barrier(jnp.sum(expo, axis=1))
            mixed = jnp.dot(expo.astype(jnp.bfloat16), values, preferred_element_type=jnp.float32)
            return mixed / total[:, None]
        return lax.map(one_head, jnp.arange(HEADS, dtype=jnp.int32))
    attended = lax.map(one_request, jnp.arange(REQS, dtype=jnp.int32))
    flat = jnp.transpose(attended, (0, 2, 1, 3)).reshape(TOKENS, HEADS * HD)
    attn = lax.dot_general(flat, w_attn[3].astype(jnp.float32), (((1,), (1,)), ((), ())), precision=lax.Precision.HIGHEST)
    hidden = (tokens.astype(jnp.float32) + attn).astype(jnp.bfloat16)
    normed2 = rms_scale(hidden, ffn_gain)
    pieces_gu = w_gate_up.reshape(N_DP, HIDDEN_PIECES, EXP_DP, D, 2 * PIECE_HIDDEN)
    pieces_dn = w_down.reshape(N_DP, HIDDEN_PIECES, EXP_DP, PIECE_HIDDEN, D)
    flat_expert = routes.reshape(-1).astype(jnp.int32)
    order = jnp.argsort(flat_expert, stable=True).astype(jnp.int32)
    attention_block = 256
    sorted_tok = jnp.concatenate([order // TOP, jnp.zeros((attention_block,), jnp.int32)])
    sorted_gain = jnp.concatenate([route_gain.reshape(-1)[order], jnp.zeros((attention_block,), jnp.float32)])
    counts = lax.optimization_barrier(jnp.sum((flat_expert[:, None] == jnp.arange(EXPERTS, dtype=jnp.int32)[None, :]).astype(jnp.int32), axis=0))
    starts = jnp.cumsum(counts) - counts

    def expert_step(expert, acc):
        owner = expert // EXP_DP
        local = expert % EXP_DP
        both = pieces_gu[owner, :, local]
        gate = jnp.transpose(both[:, :, :PIECE_HIDDEN], (1, 0, 2)).reshape(D, FF)
        upper = jnp.transpose(both[:, :, PIECE_HIDDEN:], (1, 0, 2)).reshape(D, FF)
        down_projected = pieces_dn[owner, :, local].astype(jnp.float32)

        def block_step(index, inner):
            begin = (starts[expert] + index * attention_block).astype(jnp.int32)
            rows_at = lax.dynamic_slice_in_dim(sorted_tok, begin, attention_block, 0)
            gains = lax.dynamic_slice_in_dim(sorted_gain, begin, attention_block, 0)
            valid = index * attention_block + jnp.arange(attention_block, dtype=jnp.int32) < counts[expert]
            rows = normed2[rows_at]
            activation = (jax.nn.silu(jnp.dot(rows, gate, preferred_element_type=jnp.float32)) * jnp.dot(rows, upper, preferred_element_type=jnp.float32)).astype(jnp.bfloat16)
            part_list = jnp.einsum('owu,wux->owx', activation.reshape(attention_block, HIDDEN_PIECES, PIECE_HIDDEN).astype(jnp.float32), down_projected)
            rounded = lax.optimization_barrier(part_list.astype(jnp.bfloat16))
            out = lax.optimization_barrier(jnp.sum(rounded.astype(jnp.float32), axis=1))
            weight = jnp.where(valid, gains, 0.0)
            return inner.at[rows_at].add(out * weight[:, None])
        blocks = (counts[expert] + attention_block - 1) // attention_block
        return lax.fori_loop(0, blocks, block_step, acc)
    moe = lax.fori_loop(0, EXPERTS, expert_step, jnp.zeros((TOKENS, D), jnp.float32))
    return (hidden.astype(jnp.float32) + moe).astype(jnp.bfloat16)
```

```python
import functools
import math

import jax
import jax.numpy as jnp
from jax import lax
from jax.experimental import pallas as pl
from jax.experimental.pallas import tpu as pltpu
from jax.sharding import Mesh, PartitionSpec as P

HEADS = 8
HD = 128
EXPERTS = 64
TOP = 4

rope_base = 50000.0
norm_eps = 1e-06
very_low = -1e30

GROUP = ("y", "zh", "zl")
EXPERT_AXES = ("dp", "zh", "zl")


def rms_scale(rows, gain):
    values = rows.astype(jnp.float32)
    power = jnp.mean(values * values, axis=-1, keepdims=True)
    return (values * lax.rsqrt(power + norm_eps) * gain).astype(jnp.bfloat16)


def rotate(values, positions):
    half = values.shape[-1] // 2
    freq = rope_base ** (-(jnp.arange(half, dtype=jnp.float32) * 2.0) / values.shape[-1])
    angle = positions.astype(jnp.float32)[:, None] * freq[None, :]
    cosine = jnp.cos(angle)
    sine = jnp.sin(angle)
    first = values[:, :half]
    second = values[:, half:]
    return jnp.concatenate([first * cosine - second * sine, second * cosine + first * sine], axis=1)


def attend_kernel(q_ref, kv_ref, new_ref, bias_ref, out_ref):
    q = q_ref[...]
    scale = 1.0 / math.sqrt(HD)
    old = kv_ref.shape[0]
    nt = (((1,), (1,)), ((), ()))
    s_old = lax.dot_general(q, kv_ref[:, :HD], nt, preferred_element_type=jnp.float32) * scale
    s_old = jnp.where(bias_ref[...] < 0.0, very_low, s_old)
    s_new = lax.dot_general(q, new_ref[:, :HD], nt, preferred_element_type=jnp.float32) * scale
    top = jnp.maximum(
        jnp.max(s_old, axis=1, keepdims=True), jnp.max(s_new, axis=1, keepdims=True)
    )
    top = top.astype(jnp.bfloat16).astype(jnp.float32)
    e_old = jnp.exp(s_old - top)
    e_new = jnp.exp(s_new - top)
    total = jnp.sum(e_old, axis=1, keepdims=True) + jnp.sum(e_new, axis=1, keepdims=True)
    mixed = jnp.dot(
        e_old.astype(jnp.bfloat16), kv_ref[:, HD:], preferred_element_type=jnp.float32
    ) + jnp.dot(e_new.astype(jnp.bfloat16), new_ref[:, HD:], preferred_element_type=jnp.float32)
    out_ref[:, :HD] = mixed.astype(jnp.bfloat16)
    coarse = total.astype(jnp.bfloat16).astype(jnp.float32)
    lane = lax.broadcasted_iota(jnp.int32, (q.shape[0], HD), 1)
    stats = jnp.where(lane == 0, top, jnp.where(lane == 1, coarse, total - coarse))
    out_ref[:, HD:] = stats.astype(jnp.bfloat16)


def attend(query, cached, fresh, bias):
    rows = query.shape[0]
    block = math.gcd(rows, 256)
    old, new = cached.shape[0], fresh.shape[0]
    return pl.pallas_call(
        attend_kernel,
        grid=(rows // block,),
        out_shape=jax.ShapeDtypeStruct((rows, 2 * HD), jnp.bfloat16),
        in_specs=[
            pl.BlockSpec((block, HD), lambda i: (i, 0)),
            pl.BlockSpec((old, 2 * HD), lambda i: (0, 0)),
            pl.BlockSpec((new, 2 * HD), lambda i: (0, 0)),
            pl.BlockSpec((1, old), lambda i: (0, 0)),
        ],
        out_specs=pl.BlockSpec((block, 2 * HD), lambda i: (i, 0)),
        cost_estimate=pl.CostEstimate(
            flops=4 * rows * (old + new) * HD,
            bytes_accessed=6 * (rows + old + new) * HD,
            transcendentals=rows * (old + new),
        ),
    )(query, cached, fresh, bias)


def local(
    tokens,
    attn_gain,
    ffn_gain,
    w_attn,
    kv_pool,
    page_table,
    cache_len,
    routes,
    route_gain,
    w_gate_up,
    w_down,
):
    group = lax.axis_size("y") * lax.axis_size("zh") * lax.axis_size("zl")
    split = lax.axis_size("zl")
    part = lax.axis_index("zl")
    tok_dev, width = tokens.shape
    span = tok_dev * group
    length = cache_len[0]

    sent_w = jnp.transpose(w_attn[:3], (0, 2, 1))
    head_w = lax.all_gather(sent_w, "zl", axis=1, tiled=True)
    project_w = head_w.reshape(3 * HD, width)
    normed = rms_scale(tokens, attn_gain)
    piece = lax.all_gather(normed, ("y", "zh"), axis=0, tiled=True)

    slots = kv_pool.shape[0]
    page = kv_pool.shape[2]
    sub = page // split
    sent = kv_pool.reshape(slots, HEADS * split, sub, 2 * HD)
    arrived = lax.all_to_all(sent, GROUP, split_axis=1, concat_axis=0, tiled=True)
    cached = arrived.reshape(group * slots * sub, 2 * HD)

    out_w = lax.all_gather(jnp.transpose(w_attn[3], (1, 0)), GROUP, axis=0, tiled=True)

    place_of = jnp.arange(piece.shape[0], dtype=jnp.int32)
    positions = length + (place_of // tok_dev * split + part) * tok_dev + place_of % tok_dev
    product = lax.dot_general(
        piece, project_w, (((1,), (1,)), ((), ())), preferred_element_type=jnp.float32
    )
    query = rotate(product[:, :HD], positions).astype(jnp.bfloat16)
    key_new = rotate(product[:, HD : 2 * HD], positions).astype(jnp.bfloat16)
    fresh = jnp.concatenate([key_new, product[:, 2 * HD :].astype(jnp.bfloat16)], axis=1)

    query = query.reshape(1, group // split, tok_dev, HD)
    query = jnp.broadcast_to(query, (split,) + query.shape[1:])
    query = lax.all_to_all(query, "zl", split_axis=0, concat_axis=0, tiled=True)
    query = jnp.transpose(query, (1, 0, 2, 3)).reshape(span, HD)

    table = page_table[0]
    slot_ids = jnp.arange(group * slots, dtype=jnp.int32)
    hits = table[None, :] == slot_ids[:, None]
    page_of = jnp.sum(
        jnp.where(hits, jnp.arange(table.shape[0], dtype=jnp.int32)[None, :], 0), axis=1
    )
    present = jnp.any(hits, axis=1)
    position = page_of[:, None] * page + part * sub + jnp.arange(sub, dtype=jnp.int32)[None, :]
    live = (present[:, None] & (position < length)).reshape(1, -1)
    bias = jnp.where(live, 0.0, very_low).astype(jnp.float32)

    packed = attend(query, cached, fresh, bias)
    landed_rows = lax.all_to_all(
        packed.reshape(group, tok_dev, 2 * HD), GROUP, split_axis=0, concat_axis=0, tiled=True
    ).astype(jnp.float32).reshape(HEADS, split, tok_dev, 2 * HD)
    tops = landed_rows[..., HD]
    weight = jnp.exp(tops - jnp.max(tops, axis=1, keepdims=True))
    totals = jnp.sum(weight * (landed_rows[..., HD + 1] + landed_rows[..., HD + 2]), axis=1)
    numer = jnp.sum(weight[..., None] * landed_rows[..., :HD], axis=1)
    merged = numer / totals[..., None]
    merged = jnp.transpose(merged, (1, 0, 2)).reshape(tok_dev, HEADS * HD)
    attn = jnp.dot(merged, out_w.astype(jnp.float32), precision=lax.Precision.HIGHEST)
    hidden = (tokens.astype(jnp.float32) + attn).astype(jnp.bfloat16)
    normed2 = rms_scale(hidden, ffn_gain)

    gate_up = lax.all_gather(w_gate_up, "y", axis=0, tiled=True)
    down = lax.all_gather(w_down, "y", axis=0, tiled=True)

    cap = max(2, tok_dev * TOP * 5 // (4 * EXPERTS))
    flat_expert = routes.reshape(-1)
    onehot = (flat_expert[:, None] == jnp.arange(EXPERTS, dtype=jnp.int32)[None, :]).astype(
        jnp.int32
    )
    rank = jnp.sum(jnp.cumsum(onehot, axis=0) * onehot, axis=1) - 1
    slot_id = flat_expert * cap + rank
    total_slots = EXPERTS * cap
    place = (slot_id[:, None] == jnp.arange(total_slots, dtype=jnp.int32)[None, :]).astype(
        jnp.float32
    )
    token_of = (
        jnp.arange(tok_dev * TOP, dtype=jnp.int32)[:, None] // TOP
        == jnp.arange(tok_dev, dtype=jnp.int32)[None, :]
    ).astype(jnp.float32)
    dispatch = jnp.dot(place.T, token_of, precision=lax.Precision.HIGHEST).astype(jnp.bfloat16)
    combine = jnp.dot(
        token_of.T, place * route_gain.reshape(-1)[:, None], precision=lax.Precision.HIGHEST
    )
    buffer = jnp.dot(dispatch, normed2, preferred_element_type=jnp.float32).astype(jnp.bfloat16)
    landed = lax.all_to_all(
        buffer.reshape(EXPERTS, cap, width), EXPERT_AXES, split_axis=0, concat_axis=0, tiled=True
    ).reshape(total_slots, width)

    units = w_down.shape[1]
    both = jnp.einsum("rd,qdf->qrf", landed, gate_up, preferred_element_type=jnp.float32)
    activation = (jax.nn.silu(both[..., :units]) * both[..., units:]).astype(jnp.bfloat16)
    summed = jnp.einsum("qrf,qfd->rd", activation, down, preferred_element_type=jnp.float32)
    output_rows = lax.all_to_all(
        summed.astype(jnp.bfloat16).reshape(EXPERTS, cap, width),
        EXPERT_AXES,
        split_axis=0,
        concat_axis=0,
        tiled=True,
    ).reshape(total_slots, width)
    moe = jnp.dot(combine, output_rows.astype(jnp.float32), precision=lax.Precision.HIGHEST)
    return (hidden.astype(jnp.float32) + moe).astype(jnp.bfloat16)


def solution(mesh):
    n_dp, n_tensor = mesh.devices.shape
    inner = Mesh(
        mesh.devices.reshape(n_dp, n_tensor // 8, 2, 4), ("dp", "y", "zh", "zl")
    )
    everywhere = ("dp",) + GROUP
    placed = (
        P(everywhere, None),
        P(),
        P(),
        P(None, None, GROUP),
        P(everywhere, None, None, None),
        P("dp", None),
        P("dp"),
        P(everywhere, None),
        P(everywhere, None),
        P(everywhere, None, None),
        P(everywhere, None, None),
    )
    return jax.shard_map(
        local, mesh=inner, in_specs=placed, out_specs=P(everywhere, None), check_vma=False
    )
```

```python
import functools
import math

import jax
import jax.numpy as jnp
from jax import lax
from jax.experimental import pallas as pl
from jax.experimental.pallas import tpu as pltpu
from jax.sharding import Mesh, PartitionSpec as P

HEADS = 8
HD = 128
EXPERTS = 64
TOP = 4

rope_base = 50000.0
norm_eps = 1e-06
very_low = -1e30

GROUP = ("y", "zh", "zl")
EXPERT_AXES = ("dp", "zh", "zl")


def rms_scale(rows, gain):
    values = rows.astype(jnp.float32)
    power = jnp.mean(values * values, axis=-1, keepdims=True)
    return (values * lax.rsqrt(power + norm_eps) * gain).astype(jnp.bfloat16)


def rotate(values, positions):
    half = values.shape[-1] // 2
    freq = rope_base ** (-(jnp.arange(half, dtype=jnp.float32) * 2.0) / values.shape[-1])
    angle = positions.astype(jnp.float32)[:, None] * freq[None, :]
    cosine = jnp.cos(angle)
    sine = jnp.sin(angle)
    first = values[:, :half]
    second = values[:, half:]
    return jnp.concatenate([first * cosine - second * sine, second * cosine + first * sine], axis=1)


def attend_kernel(q_ref, kv_ref, new_ref, bias_ref, out_ref):
    q = q_ref[...]
    scale = 1.0 / math.sqrt(HD)
    old = kv_ref.shape[0]
    nt = (((1,), (1,)), ((), ()))
    s_old = lax.dot_general(q, kv_ref[:, :HD], nt, preferred_element_type=jnp.float32) * scale
    s_old = jnp.where(bias_ref[...] < 0.0, very_low, s_old)
    s_new = lax.dot_general(q, new_ref[:, :HD], nt, preferred_element_type=jnp.float32) * scale
    top = jnp.maximum(
        jnp.max(s_old, axis=1, keepdims=True), jnp.max(s_new, axis=1, keepdims=True)
    )
    top = top.astype(jnp.bfloat16).astype(jnp.float32)
    e_old = jnp.exp(s_old - top)
    e_new = jnp.exp(s_new - top)
    total = jnp.sum(e_old, axis=1, keepdims=True) + jnp.sum(e_new, axis=1, keepdims=True)
    mixed = jnp.dot(
        e_old.astype(jnp.bfloat16), kv_ref[:, HD:], preferred_element_type=jnp.float32
    ) + jnp.dot(e_new.astype(jnp.bfloat16), new_ref[:, HD:], preferred_element_type=jnp.float32)
    out_ref[:, :HD] = mixed.astype(jnp.bfloat16)
    coarse = total.astype(jnp.bfloat16).astype(jnp.float32)
    lane = lax.broadcasted_iota(jnp.int32, (q.shape[0], HD), 1)
    stats = jnp.where(lane == 0, top, jnp.where(lane == 1, coarse, total - coarse))
    out_ref[:, HD:] = stats.astype(jnp.bfloat16)


def attend(query, cached, fresh, bias):
    rows = query.shape[0]
    block = math.gcd(rows, 256)
    old, new = cached.shape[0], fresh.shape[0]
    return pl.pallas_call(
        attend_kernel,
        grid=(rows // block,),
        out_shape=jax.ShapeDtypeStruct((rows, 2 * HD), jnp.bfloat16),
        in_specs=[
            pl.BlockSpec((block, HD), lambda i: (i, 0)),
            pl.BlockSpec((old, 2 * HD), lambda i: (0, 0)),
            pl.BlockSpec((new, 2 * HD), lambda i: (0, 0)),
            pl.BlockSpec((1, old), lambda i: (0, 0)),
        ],
        out_specs=pl.BlockSpec((block, 2 * HD), lambda i: (i, 0)),
        cost_estimate=pl.CostEstimate(
            flops=4 * rows * (old + new) * HD,
            bytes_accessed=6 * (rows + old + new) * HD,
            transcendentals=rows * (old + new),
        ),
    )(query, cached, fresh, bias)


def spread_kernel(
    w_ref, n_ref, kv_ref, w_out, n_out, kv_out, w_sem, n_sem, kv_send, kv_recv, own_sem
):
    n_y, n_zh, n_zl = lax.axis_size("y"), lax.axis_size("zh"), lax.axis_size("zl")
    y, zh, zl = lax.axis_index("y"), lax.axis_index("zh"), lax.axis_index("zl")
    group = n_y * n_zh * n_zl
    me = (y * n_zh + zh) * n_zl + zl
    slot = y * n_zh + zh
    over = lax.rem(zh + 1, n_zh)
    over_slot = y * n_zh + over
    sub = kv_ref.shape[2] // n_zl

    def at(member):
        return {"y": member // (n_zh * n_zl), "zh": member // n_zl % n_zh, "zl": member % n_zl}

    def copy(src, dst, send, recv, device):
        return pltpu.make_async_remote_copy(
            src_ref=src,
            dst_ref=dst,
            send_sem=send,
            recv_sem=recv,
            device_id=device,
            device_id_type=pl.DeviceIdType.MESH,
        )

    barrier = pltpu.get_barrier_semaphore()

    @pl.loop(1, group)
    def _(step):
        pl.semaphore_signal(
            barrier,
            inc=1,
            device_id=at(lax.rem(me + step, group)),
            device_id_type=pl.DeviceIdType.MESH,
        )

    pl.semaphore_wait(barrier, group - 1)

    def pages(member):
        rows = pl.ds(pl.multiple_of(member % n_zl * sub, sub), sub)
        return kv_ref.at[:, member // n_zl, rows, :]

    own = [
        pltpu.make_async_copy(w_ref, w_out.at[:, zl], own_sem.at[0]),
        pltpu.make_async_copy(n_ref, n_out.at[slot], own_sem.at[1]),
        pltpu.make_async_copy(pages(me), kv_out.at[me], own_sem.at[2]),
    ]
    across = copy(n_ref, n_out.at[slot], n_sem.at[0, 0], n_sem.at[1, slot], {"zh": over})
    across.start()
    near = []
    for step in (1, 3, 2):
        device = {"y": lax.rem(y + step, n_y)}
        near.append(
            copy(n_ref, n_out.at[slot], n_sem.at[0, step], n_sem.at[1, slot], device)
        )
        near[-1].start()
    heads = []
    for step in (1, 3, 2):
        device = {"zl": lax.rem(zl + step, n_zl)}
        heads.append(
            copy(w_ref, w_out.at[:, zl], w_sem.at[0, step], w_sem.at[1, zl], device)
        )
        heads[-1].start()
    for item in own:
        item.start()

    @pl.loop(1, group)
    def _(step):
        to = lax.rem(me + step, group)
        copy(pages(to), kv_out.at[me], kv_send.at[to], kv_recv.at[me], at(to)).start()

    copy(
        n_ref, n_out.at[over_slot], n_sem.at[0, 0], n_sem.at[1, over_slot], {"zh": over}
    ).wait_recv()
    for step in (1, 3, 2):
        device = {"y": lax.rem(y + step, n_y)}
        near.append(
            copy(
                n_out.at[over_slot],
                n_out.at[over_slot],
                n_sem.at[0, 4 + step],
                n_sem.at[1, over_slot],
                device,
            )
        )
        near[-1].start()

    for step in (1, 3, 2):
        other = lax.rem(y + step, n_y)
        for half in range(2):
            there = other * n_zh + half
            copy(
                n_ref, n_out.at[there], n_sem.at[0, 0], n_sem.at[1, there], {"y": other}
            ).wait_recv()
        there = lax.rem(zl + step, n_zl)
        copy(
            w_ref, w_out.at[:, there], w_sem.at[0, 0], w_sem.at[1, there], {"zl": there}
        ).wait_recv()

    @pl.loop(1, group)
    def _(step):
        to = lax.rem(me + step, group)
        arrival = copy(pages(to), kv_out.at[to], kv_send.at[to], kv_recv.at[to], at(to))
        arrival.wait_recv()
        arrival.wait_send()

    across.wait_send()
    for item in near + heads:
        item.wait_send()
    for item in own:
        item.wait()


def spread(sent_w, normed, kv_pool):
    n_y, n_zh, n_zl = lax.axis_size("y"), lax.axis_size("zh"), lax.axis_size("zl")
    group = n_y * n_zh * n_zl
    slots, _, page, lanes = kv_pool.shape
    kinds, cols, width = sent_w.shape
    dma = pltpu.SemaphoreType.DMA
    return pl.pallas_call(
        spread_kernel,
        out_shape=(
            jax.ShapeDtypeStruct((kinds, n_zl, cols, width), jnp.bfloat16),
            jax.ShapeDtypeStruct((n_y * n_zh,) + normed.shape, jnp.bfloat16),
            jax.ShapeDtypeStruct((group, slots, page // n_zl, lanes), jnp.bfloat16),
        ),
        in_specs=[pl.BlockSpec(memory_space=pltpu.VMEM)] * 3,
        out_specs=(pl.BlockSpec(memory_space=pl.ANY),) * 3,
        scratch_shapes=[
            dma((2, n_zl)),
            dma((2, n_y * n_zh)),
            dma((group,)),
            dma((group,)),
            dma((3,)),
        ],
        compiler_params=pltpu.CompilerParams(collective_id=0, has_side_effects=True),
        cost_estimate=pl.CostEstimate(
            flops=0, bytes_accessed=100_000_000, transcendentals=0
        ),
    )(sent_w, normed, kv_pool)


def local(
    tokens,
    attn_gain,
    ffn_gain,
    w_attn,
    kv_pool,
    page_table,
    cache_len,
    routes,
    route_gain,
    w_gate_up,
    w_down,
):
    group = lax.axis_size("y") * lax.axis_size("zh") * lax.axis_size("zl")
    split = lax.axis_size("zl")
    part = lax.axis_index("zl")
    tok_dev, width = tokens.shape
    span = tok_dev * group
    length = cache_len[0]

    sent_w = jnp.transpose(w_attn[:3], (0, 2, 1))
    normed = rms_scale(tokens, attn_gain)
    head_w, piece, arrived = spread(sent_w, normed, kv_pool)
    project_w = head_w.reshape(3 * HD, width)
    piece = piece.reshape(-1, width)

    slots = kv_pool.shape[0]
    page = kv_pool.shape[2]
    sub = page // split
    cached = arrived.reshape(group * slots * sub, 2 * HD)

    out_w = lax.all_gather(jnp.transpose(w_attn[3], (1, 0)), GROUP, axis=0, tiled=True)

    place_of = jnp.arange(piece.shape[0], dtype=jnp.int32)
    positions = length + (place_of // tok_dev * split + part) * tok_dev + place_of % tok_dev
    product = lax.dot_general(
        piece, project_w, (((1,), (1,)), ((), ())), preferred_element_type=jnp.float32
    )
    query = rotate(product[:, :HD], positions).astype(jnp.bfloat16)
    key_new = rotate(product[:, HD : 2 * HD], positions).astype(jnp.bfloat16)
    fresh = jnp.concatenate([key_new, product[:, 2 * HD :].astype(jnp.bfloat16)], axis=1)

    query = query.reshape(1, group // split, tok_dev, HD)
    query = jnp.broadcast_to(query, (split,) + query.shape[1:])
    query = lax.all_to_all(query, "zl", split_axis=0, concat_axis=0, tiled=True)
    query = jnp.transpose(query, (1, 0, 2, 3)).reshape(span, HD)

    table = page_table[0]
    slot_ids = jnp.arange(group * slots, dtype=jnp.int32)
    hits = table[None, :] == slot_ids[:, None]
    page_of = jnp.sum(
        jnp.where(hits, jnp.arange(table.shape[0], dtype=jnp.int32)[None, :], 0), axis=1
    )
    present = jnp.any(hits, axis=1)
    position = page_of[:, None] * page + part * sub + jnp.arange(sub, dtype=jnp.int32)[None, :]
    live = (present[:, None] & (position < length)).reshape(1, -1)
    bias = jnp.where(live, 0.0, very_low).astype(jnp.float32)

    packed = attend(query, cached, fresh, bias)
    landed_rows = lax.all_to_all(
        packed.reshape(group, tok_dev, 2 * HD), GROUP, split_axis=0, concat_axis=0, tiled=True
    ).astype(jnp.float32).reshape(HEADS, split, tok_dev, 2 * HD)
    tops = landed_rows[..., HD]
    weight = jnp.exp(tops - jnp.max(tops, axis=1, keepdims=True))
    totals = jnp.sum(weight * (landed_rows[..., HD + 1] + landed_rows[..., HD + 2]), axis=1)
    numer = jnp.sum(weight[..., None] * landed_rows[..., :HD], axis=1)
    merged = numer / totals[..., None]
    merged = jnp.transpose(merged, (1, 0, 2)).reshape(tok_dev, HEADS * HD)
    attn = jnp.dot(merged, out_w.astype(jnp.float32), precision=lax.Precision.HIGHEST)
    hidden = (tokens.astype(jnp.float32) + attn).astype(jnp.bfloat16)
    normed2 = rms_scale(hidden, ffn_gain)

    gate_up = lax.all_gather(w_gate_up, "y", axis=0, tiled=True)
    down = lax.all_gather(w_down, "y", axis=0, tiled=True)

    cap = max(2, tok_dev * TOP * 5 // (4 * EXPERTS))
    flat_expert = routes.reshape(-1)
    onehot = (flat_expert[:, None] == jnp.arange(EXPERTS, dtype=jnp.int32)[None, :]).astype(
        jnp.int32
    )
    rank = jnp.sum(jnp.cumsum(onehot, axis=0) * onehot, axis=1) - 1
    slot_id = flat_expert * cap + rank
    total_slots = EXPERTS * cap
    place = (slot_id[:, None] == jnp.arange(total_slots, dtype=jnp.int32)[None, :]).astype(
        jnp.float32
    )
    token_of = (
        jnp.arange(tok_dev * TOP, dtype=jnp.int32)[:, None] // TOP
        == jnp.arange(tok_dev, dtype=jnp.int32)[None, :]
    ).astype(jnp.float32)
    dispatch = jnp.dot(place.T, token_of, precision=lax.Precision.HIGHEST).astype(jnp.bfloat16)
    combine = jnp.dot(
        token_of.T, place * route_gain.reshape(-1)[:, None], precision=lax.Precision.HIGHEST
    )
    buffer = jnp.dot(dispatch, normed2, preferred_element_type=jnp.float32).astype(jnp.bfloat16)
    landed = lax.all_to_all(
        buffer.reshape(EXPERTS, cap, width), EXPERT_AXES, split_axis=0, concat_axis=0, tiled=True
    ).reshape(total_slots, width)

    units = w_down.shape[1]
    both = jnp.einsum("rd,qdf->qrf", landed, gate_up, preferred_element_type=jnp.float32)
    activation = (jax.nn.silu(both[..., :units]) * both[..., units:]).astype(jnp.bfloat16)
    summed = jnp.einsum("qrf,qfd->rd", activation, down, preferred_element_type=jnp.float32)
    output_rows = lax.all_to_all(
        summed.astype(jnp.bfloat16).reshape(EXPERTS, cap, width),
        EXPERT_AXES,
        split_axis=0,
        concat_axis=0,
        tiled=True,
    ).reshape(total_slots, width)
    moe = jnp.dot(combine, output_rows.astype(jnp.float32), precision=lax.Precision.HIGHEST)
    return (hidden.astype(jnp.float32) + moe).astype(jnp.bfloat16)


def solution(mesh):
    n_dp, n_tensor = mesh.devices.shape
    inner = Mesh(
        mesh.devices.reshape(n_dp, n_tensor // 8, 2, 4), ("dp", "y", "zh", "zl")
    )
    everywhere = ("dp",) + GROUP
    placed = (
        P(everywhere, None),
        P(),
        P(),
        P(None, None, GROUP),
        P(everywhere, None, None, None),
        P("dp", None),
        P("dp"),
        P(everywhere, None),
        P(everywhere, None),
        P(everywhere, None, None),
        P(everywhere, None, None),
    )
    return jax.shard_map(
        local, mesh=inner, in_specs=placed, out_specs=P(everywhere, None), check_vma=False
    )
```

```python
import functools
import math

import jax
import jax.numpy as jnp
from jax import lax
from jax.experimental import pallas as pl
from jax.experimental.pallas import tpu as pltpu
from jax.sharding import Mesh, PartitionSpec as P

HEADS = 8
HD = 128
EXPERTS = 64
TOP = 4

rope_base = 50000.0
norm_eps = 1e-06
very_low = -1e30

GROUP = ("y", "zh", "zl")
EXPERT_AXES = ("dp", "zh", "zl")


def rms_scale(rows, gain):
    values = rows.astype(jnp.float32)
    power = jnp.mean(values * values, axis=-1, keepdims=True)
    return (values * lax.rsqrt(power + norm_eps) * gain).astype(jnp.bfloat16)


def rotate(values, positions):
    half = values.shape[-1] // 2
    freq = rope_base ** (-(jnp.arange(half, dtype=jnp.float32) * 2.0) / values.shape[-1])
    angle = positions.astype(jnp.float32)[:, None] * freq[None, :]
    cosine = jnp.cos(angle)
    sine = jnp.sin(angle)
    first = values[:, :half]
    second = values[:, half:]
    return jnp.concatenate([first * cosine - second * sine, second * cosine + first * sine], axis=1)


def attend_kernel(q_ref, kv_ref, new_ref, bias_ref, out_ref):
    q = q_ref[...]
    scale = 1.0 / math.sqrt(HD)
    old = kv_ref.shape[0]
    nt = (((1,), (1,)), ((), ()))
    s_old = lax.dot_general(q, kv_ref[:, :HD], nt, preferred_element_type=jnp.float32) * scale
    s_old = jnp.where(bias_ref[...] < 0.0, very_low, s_old)
    s_new = lax.dot_general(q, new_ref[:, :HD], nt, preferred_element_type=jnp.float32) * scale
    top = jnp.maximum(
        jnp.max(s_old, axis=1, keepdims=True), jnp.max(s_new, axis=1, keepdims=True)
    )
    top = top.astype(jnp.bfloat16).astype(jnp.float32)
    e_old = jnp.exp(s_old - top)
    e_new = jnp.exp(s_new - top)
    total = jnp.sum(e_old, axis=1, keepdims=True) + jnp.sum(e_new, axis=1, keepdims=True)
    mixed = jnp.dot(
        e_old.astype(jnp.bfloat16), kv_ref[:, HD:], preferred_element_type=jnp.float32
    ) + jnp.dot(e_new.astype(jnp.bfloat16), new_ref[:, HD:], preferred_element_type=jnp.float32)
    out_ref[:, :HD] = mixed.astype(jnp.bfloat16)
    coarse = total.astype(jnp.bfloat16).astype(jnp.float32)
    lane = lax.broadcasted_iota(jnp.int32, (q.shape[0], HD), 1)
    stats = jnp.where(lane == 0, top, jnp.where(lane == 1, coarse, total - coarse))
    out_ref[:, HD:] = stats.astype(jnp.bfloat16)


def attend(query, cached, fresh, bias):
    rows = query.shape[0]
    block = math.gcd(rows, 256)
    old, new = cached.shape[0], fresh.shape[0]
    return pl.pallas_call(
        attend_kernel,
        grid=(rows // block,),
        out_shape=jax.ShapeDtypeStruct((rows, 2 * HD), jnp.bfloat16),
        in_specs=[
            pl.BlockSpec((block, HD), lambda i: (i, 0)),
            pl.BlockSpec((old, 2 * HD), lambda i: (0, 0)),
            pl.BlockSpec((new, 2 * HD), lambda i: (0, 0)),
            pl.BlockSpec((1, old), lambda i: (0, 0)),
        ],
        out_specs=pl.BlockSpec((block, 2 * HD), lambda i: (i, 0)),
        cost_estimate=pl.CostEstimate(
            flops=4 * rows * (old + new) * HD,
            bytes_accessed=6 * (rows + old + new) * HD,
            transcendentals=rows * (old + new),
        ),
    )(query, cached, fresh, bias)


def spread_kernel(
    w_ref,
    n_ref,
    kv_ref,
    w_out,
    n_out,
    kv_out,
    w_sem,
    dp_sem,
    n_sem,
    kv_send,
    kv_recv,
    own_sem,
):
    n_y, n_zh, n_zl = lax.axis_size("y"), lax.axis_size("zh"), lax.axis_size("zl")
    y, zh, zl = lax.axis_index("y"), lax.axis_index("zh"), lax.axis_index("zl")
    group = n_y * n_zh * n_zl
    me = (y * n_zh + zh) * n_zl + zl
    slot = y * n_zh + zh
    over = lax.rem(zh + 1, n_zh)
    over_slot = y * n_zh + over
    sub = kv_ref.shape[2] // n_zl
    n_dp, dp = lax.axis_size("dp"), lax.axis_index("dp")
    stripe = w_ref.shape[2]

    def columns(which):
        return pl.ds(pl.multiple_of(which * stripe, stripe), stripe)

    def at(member):
        return {"y": member // (n_zh * n_zl), "zh": member // n_zl % n_zh, "zl": member % n_zl}

    def copy(src, dst, send, recv, device):
        return pltpu.make_async_remote_copy(
            src_ref=src,
            dst_ref=dst,
            send_sem=send,
            recv_sem=recv,
            device_id=device,
            device_id_type=pl.DeviceIdType.MESH,
        )

    barrier = pltpu.get_barrier_semaphore()

    @pl.loop(1, group)
    def _(step):
        pl.semaphore_signal(
            barrier,
            inc=1,
            device_id=at(lax.rem(me + step, group)),
            device_id_type=pl.DeviceIdType.MESH,
        )

    @pl.loop(1, n_dp)
    def _(step):
        pl.semaphore_signal(
            barrier,
            inc=1,
            device_id={"dp": lax.rem(dp + step, n_dp)},
            device_id_type=pl.DeviceIdType.MESH,
        )

    pl.semaphore_wait(barrier, group + n_dp - 2)

    def pages(member):
        rows = pl.ds(pl.multiple_of(member % n_zl * sub, sub), sub)
        return kv_ref.at[:, member // n_zl, rows, :]

    own = [
        pltpu.make_async_copy(w_ref, w_out.at[:, zl, :, columns(dp)], own_sem.at[0]),
        pltpu.make_async_copy(n_ref, n_out.at[slot], own_sem.at[1]),
        pltpu.make_async_copy(pages(me), kv_out.at[me], own_sem.at[2]),
    ]
    across = copy(n_ref, n_out.at[slot], n_sem.at[0, 0], n_sem.at[1, slot], {"zh": over})
    across.start()
    near = []
    for step in (1, 3, 2):
        device = {"y": lax.rem(y + step, n_y)}
        near.append(
            copy(n_ref, n_out.at[slot], n_sem.at[0, step], n_sem.at[1, slot], device)
        )
        near[-1].start()
    heads = []
    for step in (1, 3, 2):
        device = {"zl": lax.rem(zl + step, n_zl)}
        heads.append(
            copy(
                w_ref,
                w_out.at[:, zl, :, columns(dp)],
                w_sem.at[0, step],
                w_sem.at[1, zl],
                device,
            )
        )
        heads[-1].start()
    for item in own:
        item.start()

    @pl.loop(1, group)
    def _(step):
        to = lax.rem(me + step, group)
        copy(pages(to), kv_out.at[me], kv_send.at[to], kv_recv.at[me], at(to)).start()

    copy(
        n_ref, n_out.at[over_slot], n_sem.at[0, 0], n_sem.at[1, over_slot], {"zh": over}
    ).wait_recv()
    for step in (1, 3, 2):
        device = {"y": lax.rem(y + step, n_y)}
        near.append(
            copy(
                n_out.at[over_slot],
                n_out.at[over_slot],
                n_sem.at[0, 4 + step],
                n_sem.at[1, over_slot],
                device,
            )
        )
        near[-1].start()

    own[0].wait()
    for step in (1, 3, 2):
        there = lax.rem(zl + step, n_zl)
        copy(
            w_ref,
            w_out.at[:, there, :, columns(dp)],
            w_sem.at[0, 0],
            w_sem.at[1, there],
            {"zl": there},
        ).wait_recv()

    def stripes(to, which):
        return copy(
            w_out.at[:, :, :, columns(which)],
            w_out.at[:, :, :, columns(which)],
            dp_sem.at[0, to],
            dp_sem.at[1, which],
            {"dp": to},
        )

    @pl.loop(1, n_dp)
    def _(step):
        stripes(lax.rem(dp + step, n_dp), dp).start()

    for step in (1, 3, 2):
        other = lax.rem(y + step, n_y)
        for half in range(2):
            there = other * n_zh + half
            copy(
                n_ref, n_out.at[there], n_sem.at[0, 0], n_sem.at[1, there], {"y": other}
            ).wait_recv()

    @pl.loop(1, group)
    def _(step):
        to = lax.rem(me + step, group)
        arrival = copy(pages(to), kv_out.at[to], kv_send.at[to], kv_recv.at[to], at(to))
        arrival.wait_recv()
        arrival.wait_send()

    @pl.loop(1, n_dp)
    def _(step):
        other = lax.rem(dp + step, n_dp)
        stripes(other, other).wait_recv()
        stripes(other, dp).wait_send()

    across.wait_send()
    for item in near + heads:
        item.wait_send()
    for item in own[1:]:
        item.wait()


def spread(sent_w, normed, kv_pool):
    n_y, n_zh, n_zl = lax.axis_size("y"), lax.axis_size("zh"), lax.axis_size("zl")
    group = n_y * n_zh * n_zl
    slots, _, page, lanes = kv_pool.shape
    kinds, cols, stripe = sent_w.shape
    n_dp = lax.axis_size("dp")
    dma = pltpu.SemaphoreType.DMA
    return pl.pallas_call(
        spread_kernel,
        out_shape=(
            jax.ShapeDtypeStruct((kinds, n_zl, cols, n_dp * stripe), jnp.bfloat16),
            jax.ShapeDtypeStruct((n_y * n_zh,) + normed.shape, jnp.bfloat16),
            jax.ShapeDtypeStruct((group, slots, page // n_zl, lanes), jnp.bfloat16),
        ),
        in_specs=[pl.BlockSpec(memory_space=pltpu.VMEM)] * 3,
        out_specs=(pl.BlockSpec(memory_space=pl.ANY),) * 3,
        scratch_shapes=[
            dma((2, n_zl)),
            dma((2, n_dp)),
            dma((2, n_y * n_zh)),
            dma((group,)),
            dma((group,)),
            dma((3,)),
        ],
        compiler_params=pltpu.CompilerParams(collective_id=0, has_side_effects=True),
        cost_estimate=pl.CostEstimate(
            flops=0, bytes_accessed=100_000_000, transcendentals=0
        ),
    )(sent_w, normed, kv_pool)


def exchange_kernel(axes, in_ref, out_ref, send, recv, own_sem):
    sizes = [lax.axis_size(axis) for axis in axes]
    group = math.prod(sizes)
    me = 0
    for axis, size in zip(axes, sizes):
        me = me * size + lax.axis_index(axis)

    def at(member):
        device = {}
        for axis, size in reversed(list(zip(axes, sizes))):
            device[axis] = member % size
            member = member // size
        return device

    barrier = pltpu.get_barrier_semaphore()

    @pl.loop(1, group)
    def _(step):
        pl.semaphore_signal(
            barrier,
            inc=1,
            device_id=at(lax.rem(me + step, group)),
            device_id_type=pl.DeviceIdType.MESH,
        )

    pl.semaphore_wait(barrier, group - 1)
    own = pltpu.make_async_copy(in_ref.at[me], out_ref.at[me], own_sem)
    own.start()

    def copy(to, slot):
        return pltpu.make_async_remote_copy(
            src_ref=in_ref.at[to],
            dst_ref=out_ref.at[slot],
            send_sem=send.at[to],
            recv_sem=recv.at[slot],
            device_id=at(to),
            device_id_type=pl.DeviceIdType.MESH,
        )

    @pl.loop(1, group)
    def _(step):
        copy(lax.rem(me + step, group), me).start()

    @pl.loop(1, group)
    def _(step):
        to = lax.rem(me + step, group)
        arrival = copy(to, to)
        arrival.wait_recv()
        arrival.wait_send()

    own.wait()


def exchange(blocks, axes, collective_id):
    group = blocks.shape[0]
    dma = pltpu.SemaphoreType.DMA
    return pl.pallas_call(
        functools.partial(exchange_kernel, axes),
        out_shape=jax.ShapeDtypeStruct(blocks.shape, blocks.dtype),
        in_specs=[pl.BlockSpec(memory_space=pltpu.VMEM)],
        out_specs=pl.BlockSpec(memory_space=pl.ANY),
        scratch_shapes=[dma((group,)), dma((group,)), dma],
        compiler_params=pltpu.CompilerParams(
            collective_id=collective_id, has_side_effects=True
        ),
        cost_estimate=pl.CostEstimate(flops=0, bytes_accessed=60_000_000, transcendentals=0),
    )(blocks)


def local(
    tokens,
    attn_gain,
    ffn_gain,
    w_attn,
    kv_pool,
    page_table,
    cache_len,
    routes,
    route_gain,
    w_gate_up,
    w_down,
):
    group = lax.axis_size("y") * lax.axis_size("zh") * lax.axis_size("zl")
    split = lax.axis_size("zl")
    part = lax.axis_index("zl")
    tok_dev, width = tokens.shape
    span = tok_dev * group
    length = cache_len[0]

    n_dp = lax.axis_size("dp")
    stripe = width // n_dp
    own_w = lax.dynamic_slice_in_dim(w_attn, lax.axis_index("dp") * stripe, stripe, 1)
    own_w = jnp.transpose(own_w, (0, 2, 1))
    sent_w = own_w[:3]
    normed = rms_scale(tokens, attn_gain)
    head_w, piece, arrived = spread(sent_w, normed, kv_pool)
    project_w = head_w.reshape(3 * HD, width)
    piece = piece.reshape(-1, width)

    slots = kv_pool.shape[0]
    page = kv_pool.shape[2]
    sub = page // split
    cached = arrived.reshape(group * slots * sub, 2 * HD)

    out_w = lax.all_gather(own_w[3], GROUP, axis=0, tiled=True)
    out_w = lax.all_gather(out_w, "dp", axis=0)

    place_of = jnp.arange(piece.shape[0], dtype=jnp.int32)
    positions = length + (place_of // tok_dev * split + part) * tok_dev + place_of % tok_dev
    product = lax.dot_general(
        piece, project_w, (((1,), (1,)), ((), ())), preferred_element_type=jnp.float32
    )
    query = rotate(product[:, :HD], positions).astype(jnp.bfloat16)
    key_new = rotate(product[:, HD : 2 * HD], positions).astype(jnp.bfloat16)
    fresh = jnp.concatenate([key_new, product[:, 2 * HD :].astype(jnp.bfloat16)], axis=1)

    query = query.reshape(1, group // split, tok_dev, HD)
    query = jnp.broadcast_to(query, (split,) + query.shape[1:])
    query = lax.all_to_all(query, "zl", split_axis=0, concat_axis=0, tiled=True)
    query = jnp.transpose(query, (1, 0, 2, 3)).reshape(span, HD)

    table = page_table[0]
    slot_ids = jnp.arange(group * slots, dtype=jnp.int32)
    hits = table[None, :] == slot_ids[:, None]
    page_of = jnp.sum(
        jnp.where(hits, jnp.arange(table.shape[0], dtype=jnp.int32)[None, :], 0), axis=1
    )
    present = jnp.any(hits, axis=1)
    position = page_of[:, None] * page + part * sub + jnp.arange(sub, dtype=jnp.int32)[None, :]
    live = (present[:, None] & (position < length)).reshape(1, -1)
    bias = jnp.where(live, 0.0, very_low).astype(jnp.float32)

    packed = attend(query, cached, fresh, bias)
    landed_rows = exchange(packed.reshape(group, tok_dev, 2 * HD), GROUP, 1).astype(jnp.float32).reshape(HEADS, split, tok_dev, 2 * HD)
    tops = landed_rows[..., HD]
    weight = jnp.exp(tops - jnp.max(tops, axis=1, keepdims=True))
    totals = jnp.sum(weight * (landed_rows[..., HD + 1] + landed_rows[..., HD + 2]), axis=1)
    numer = jnp.sum(weight[..., None] * landed_rows[..., :HD], axis=1)
    merged = numer / totals[..., None]
    merged = jnp.transpose(merged, (1, 0, 2)).reshape(tok_dev, HEADS * HD)
    attn = jnp.einsum(
        "tk,dkn->tdn", merged, out_w.astype(jnp.float32), precision=lax.Precision.HIGHEST
    ).reshape(tok_dev, width)
    hidden = (tokens.astype(jnp.float32) + attn).astype(jnp.bfloat16)
    normed2 = rms_scale(hidden, ffn_gain)

    gate_up = lax.all_gather(w_gate_up, "y", axis=0, tiled=True)
    down = lax.all_gather(w_down, "y", axis=0, tiled=True)

    cap = max(2, tok_dev * TOP * 5 // (4 * EXPERTS))
    flat_expert = routes.reshape(-1)
    onehot = (flat_expert[:, None] == jnp.arange(EXPERTS, dtype=jnp.int32)[None, :]).astype(
        jnp.int32
    )
    rank = jnp.sum(jnp.cumsum(onehot, axis=0) * onehot, axis=1) - 1
    slot_id = flat_expert * cap + rank
    total_slots = EXPERTS * cap
    place = (slot_id[:, None] == jnp.arange(total_slots, dtype=jnp.int32)[None, :]).astype(
        jnp.float32
    )
    token_of = (
        jnp.arange(tok_dev * TOP, dtype=jnp.int32)[:, None] // TOP
        == jnp.arange(tok_dev, dtype=jnp.int32)[None, :]
    ).astype(jnp.float32)
    dispatch = jnp.dot(place.T, token_of, precision=lax.Precision.HIGHEST).astype(jnp.bfloat16)
    combine = jnp.dot(
        token_of.T, place * route_gain.reshape(-1)[:, None], precision=lax.Precision.HIGHEST
    )
    buffer = jnp.dot(dispatch, normed2, preferred_element_type=jnp.float32).astype(jnp.bfloat16)
    landed = exchange(
        buffer.reshape(EXPERTS, cap, width // HD, HD), EXPERT_AXES, 2
    ).reshape(total_slots, width)

    units = w_down.shape[1]
    both = jnp.einsum("rd,qdf->qrf", landed, gate_up, preferred_element_type=jnp.float32)
    activation = (jax.nn.silu(both[..., :units]) * both[..., units:]).astype(jnp.bfloat16)
    summed = jnp.einsum("qrf,qfd->rd", activation, down, preferred_element_type=jnp.float32)
    output_rows = exchange(
        summed.astype(jnp.bfloat16).reshape(EXPERTS, cap, width // HD, HD), EXPERT_AXES, 3
    ).reshape(total_slots, width)
    moe = jnp.dot(combine, output_rows.astype(jnp.float32), precision=lax.Precision.HIGHEST)
    return (hidden.astype(jnp.float32) + moe).astype(jnp.bfloat16)


def solution(mesh):
    n_dp, n_tensor = mesh.devices.shape
    inner = Mesh(
        mesh.devices.reshape(n_dp, n_tensor // 8, 2, 4), ("dp", "y", "zh", "zl")
    )
    everywhere = ("dp",) + GROUP
    placed = (
        P(everywhere, None),
        P(),
        P(),
        P(None, None, GROUP),
        P(everywhere, None, None, None),
        P("dp", None),
        P("dp"),
        P(everywhere, None),
        P(everywhere, None),
        P(everywhere, None, None),
        P(everywhere, None, None),
    )
    return jax.shard_map(
        local, mesh=inner, in_specs=placed, out_specs=P(everywhere, None), check_vma=False
    )
```

```python
import functools
import math

import jax
import jax.numpy as jnp
from jax import lax
from jax.experimental import pallas as pl
from jax.experimental.pallas import tpu as pltpu
from jax.sharding import Mesh, PartitionSpec as P

HEADS = 8
HD = 128
EXPERTS = 64
TOP = 4

rope_base = 50000.0
norm_eps = 1e-06
very_low = -1e30

GROUP = ("y", "zh", "zl")
EXPERT_AXES = ("dp", "zh", "zl")


def rms_scale(rows, gain):
    values = rows.astype(jnp.float32)
    power = jnp.mean(values * values, axis=-1, keepdims=True)
    return (values * lax.rsqrt(power + norm_eps) * gain).astype(jnp.bfloat16)


def rotate(values, positions):
    half = values.shape[-1] // 2
    freq = rope_base ** (-(jnp.arange(half, dtype=jnp.float32) * 2.0) / values.shape[-1])
    angle = positions.astype(jnp.float32)[:, None] * freq[None, :]
    cosine = jnp.cos(angle)
    sine = jnp.sin(angle)
    first = values[:, :half]
    second = values[:, half:]
    return jnp.concatenate([first * cosine - second * sine, second * cosine + first * sine], axis=1)


def attend_kernel(q_ref, kv_ref, new_ref, bias_ref, out_ref):
    q = q_ref[...]
    scale = 1.0 / math.sqrt(HD)
    old = kv_ref.shape[0]
    nt = (((1,), (1,)), ((), ()))
    s_old = lax.dot_general(q, kv_ref[:, :HD], nt, preferred_element_type=jnp.float32) * scale
    s_old = jnp.where(bias_ref[...] < 0.0, very_low, s_old)
    s_new = lax.dot_general(q, new_ref[:, :HD], nt, preferred_element_type=jnp.float32) * scale
    top = jnp.maximum(
        jnp.max(s_old, axis=1, keepdims=True), jnp.max(s_new, axis=1, keepdims=True)
    )
    top = top.astype(jnp.bfloat16).astype(jnp.float32)
    e_old = jnp.exp(s_old - top)
    e_new = jnp.exp(s_new - top)
    total = jnp.sum(e_old, axis=1, keepdims=True) + jnp.sum(e_new, axis=1, keepdims=True)
    mixed = jnp.dot(
        e_old.astype(jnp.bfloat16), kv_ref[:, HD:], preferred_element_type=jnp.float32
    ) + jnp.dot(e_new.astype(jnp.bfloat16), new_ref[:, HD:], preferred_element_type=jnp.float32)
    out_ref[:, :HD] = mixed.astype(jnp.bfloat16)
    coarse = total.astype(jnp.bfloat16).astype(jnp.float32)
    lane = lax.broadcasted_iota(jnp.int32, (q.shape[0], HD), 1)
    stats = jnp.where(lane == 0, top, jnp.where(lane == 1, coarse, total - coarse))
    out_ref[:, HD:] = stats.astype(jnp.bfloat16)


def attend(query, cached, fresh, bias):
    rows = query.shape[0]
    block = math.gcd(rows, 256)
    old, new = cached.shape[0], fresh.shape[0]
    return pl.pallas_call(
        attend_kernel,
        grid=(rows // block,),
        out_shape=jax.ShapeDtypeStruct((rows, 2 * HD), jnp.bfloat16),
        in_specs=[
            pl.BlockSpec((block, HD), lambda i: (i, 0)),
            pl.BlockSpec((old, 2 * HD), lambda i: (0, 0)),
            pl.BlockSpec((new, 2 * HD), lambda i: (0, 0)),
            pl.BlockSpec((1, old), lambda i: (0, 0)),
        ],
        out_specs=pl.BlockSpec((block, 2 * HD), lambda i: (i, 0)),
        cost_estimate=pl.CostEstimate(
            flops=4 * rows * (old + new) * HD,
            bytes_accessed=6 * (rows + old + new) * HD,
            transcendentals=rows * (old + new),
        ),
    )(query, cached, fresh, bias)


def spread_kernel(
    w_ref,
    n_ref,
    kv_ref,
    o_ref,
    w_out,
    n_out,
    kv_out,
    o_out,
    w_sem,
    dp_sem,
    n_sem,
    kv_send,
    kv_recv,
    o_send,
    o_recv,
    own_sem,
):
    n_y, n_zh, n_zl = lax.axis_size("y"), lax.axis_size("zh"), lax.axis_size("zl")
    y, zh, zl = lax.axis_index("y"), lax.axis_index("zh"), lax.axis_index("zl")
    group = n_y * n_zh * n_zl
    me = (y * n_zh + zh) * n_zl + zl
    slot = y * n_zh + zh
    over = lax.rem(zh + 1, n_zh)
    over_slot = y * n_zh + over
    sub = kv_ref.shape[2] // n_zl
    n_dp, dp = lax.axis_size("dp"), lax.axis_index("dp")
    stripe = w_ref.shape[2]

    def columns(which):
        return pl.ds(pl.multiple_of(which * stripe, stripe), stripe)

    def at(member):
        return {"y": member // (n_zh * n_zl), "zh": member // n_zl % n_zh, "zl": member % n_zl}

    def copy(src, dst, send, recv, device):
        return pltpu.make_async_remote_copy(
            src_ref=src,
            dst_ref=dst,
            send_sem=send,
            recv_sem=recv,
            device_id=device,
            device_id_type=pl.DeviceIdType.MESH,
        )

    barrier = pltpu.get_barrier_semaphore()

    @pl.loop(1, group)
    def _(step):
        pl.semaphore_signal(
            barrier,
            inc=1,
            device_id=at(lax.rem(me + step, group)),
            device_id_type=pl.DeviceIdType.MESH,
        )

    @pl.loop(1, n_dp)
    def _(step):
        pl.semaphore_signal(
            barrier,
            inc=1,
            device_id={"dp": lax.rem(dp + step, n_dp)},
            device_id_type=pl.DeviceIdType.MESH,
        )

    pl.semaphore_wait(barrier, group + n_dp - 2)

    def pages(member):
        rows = pl.ds(pl.multiple_of(member % n_zl * sub, sub), sub)
        return kv_ref.at[:, member // n_zl, rows, :]

    own = [
        pltpu.make_async_copy(w_ref, w_out.at[:, zl, :, columns(dp)], own_sem.at[0]),
        pltpu.make_async_copy(n_ref, n_out.at[slot], own_sem.at[1]),
        pltpu.make_async_copy(pages(me), kv_out.at[me], own_sem.at[2]),
        pltpu.make_async_copy(o_ref, o_out.at[me], own_sem.at[3]),
    ]
    across = copy(n_ref, n_out.at[slot], n_sem.at[0, 0], n_sem.at[1, slot], {"zh": over})
    across.start()
    near = []
    for step in (1, 3, 2):
        device = {"y": lax.rem(y + step, n_y)}
        near.append(
            copy(n_ref, n_out.at[slot], n_sem.at[0, step], n_sem.at[1, slot], device)
        )
        near[-1].start()
    heads = []
    for step in (1, 3, 2):
        device = {"zl": lax.rem(zl + step, n_zl)}
        heads.append(
            copy(
                w_ref,
                w_out.at[:, zl, :, columns(dp)],
                w_sem.at[0, step],
                w_sem.at[1, zl],
                device,
            )
        )
        heads[-1].start()
    for item in own:
        item.start()

    @pl.loop(1, group)
    def _(step):
        to = lax.rem(me + step, group)
        copy(pages(to), kv_out.at[me], kv_send.at[to], kv_recv.at[me], at(to)).start()
        copy(o_ref, o_out.at[me], o_send.at[to], o_recv.at[me], at(to)).start()

    copy(
        n_ref, n_out.at[over_slot], n_sem.at[0, 0], n_sem.at[1, over_slot], {"zh": over}
    ).wait_recv()
    for step in (1, 3, 2):
        device = {"y": lax.rem(y + step, n_y)}
        near.append(
            copy(
                n_out.at[over_slot],
                n_out.at[over_slot],
                n_sem.at[0, 4 + step],
                n_sem.at[1, over_slot],
                device,
            )
        )
        near[-1].start()

    own[0].wait()
    for step in (1, 3, 2):
        there = lax.rem(zl + step, n_zl)
        copy(
            w_ref,
            w_out.at[:, there, :, columns(dp)],
            w_sem.at[0, 0],
            w_sem.at[1, there],
            {"zl": there},
        ).wait_recv()

    def stripes(to, which):
        return copy(
            w_out.at[:, :, :, columns(which)],
            w_out.at[:, :, :, columns(which)],
            dp_sem.at[0, to],
            dp_sem.at[1, which],
            {"dp": to},
        )

    @pl.loop(1, n_dp)
    def _(step):
        stripes(lax.rem(dp + step, n_dp), dp).start()

    for step in (1, 3, 2):
        other = lax.rem(y + step, n_y)
        for half in range(2):
            there = other * n_zh + half
            copy(
                n_ref, n_out.at[there], n_sem.at[0, 0], n_sem.at[1, there], {"y": other}
            ).wait_recv()

    @pl.loop(1, group)
    def _(step):
        to = lax.rem(me + step, group)
        arrival = copy(pages(to), kv_out.at[to], kv_send.at[to], kv_recv.at[to], at(to))
        arrival.wait_recv()
        arrival.wait_send()
        arrival = copy(o_ref, o_out.at[to], o_send.at[to], o_recv.at[to], at(to))
        arrival.wait_recv()
        arrival.wait_send()

    @pl.loop(1, n_dp)
    def _(step):
        other = lax.rem(dp + step, n_dp)
        stripes(other, other).wait_recv()
        stripes(other, dp).wait_send()

    across.wait_send()
    for item in near + heads:
        item.wait_send()
    for item in own[1:]:
        item.wait()


def spread(sent_w, normed, kv_pool, sent_o):
    n_y, n_zh, n_zl = lax.axis_size("y"), lax.axis_size("zh"), lax.axis_size("zl")
    group = n_y * n_zh * n_zl
    slots, _, page, lanes = kv_pool.shape
    kinds, cols, stripe = sent_w.shape
    n_dp = lax.axis_size("dp")
    dma = pltpu.SemaphoreType.DMA
    return pl.pallas_call(
        spread_kernel,
        out_shape=(
            jax.ShapeDtypeStruct((kinds, n_zl, cols, n_dp * stripe), jnp.bfloat16),
            jax.ShapeDtypeStruct((n_y * n_zh,) + normed.shape, jnp.bfloat16),
            jax.ShapeDtypeStruct((group, slots, page // n_zl, lanes), jnp.bfloat16),
            jax.ShapeDtypeStruct((group,) + sent_o.shape, jnp.bfloat16),
        ),
        in_specs=[pl.BlockSpec(memory_space=pltpu.VMEM)] * 4,
        out_specs=(pl.BlockSpec(memory_space=pl.ANY),) * 4,
        scratch_shapes=[
            dma((2, n_zl)),
            dma((2, n_dp)),
            dma((2, n_y * n_zh)),
            dma((group,)),
            dma((group,)),
            dma((group,)),
            dma((group,)),
            dma((4,)),
        ],
        compiler_params=pltpu.CompilerParams(collective_id=0, has_side_effects=True),
        cost_estimate=pl.CostEstimate(
            flops=0, bytes_accessed=100_000_000, transcendentals=0
        ),
    )(sent_w, normed, kv_pool, sent_o)


def exchange_kernel(axes, in_ref, out_ref, send, recv, own_sem):
    sizes = [lax.axis_size(axis) for axis in axes]
    group = math.prod(sizes)
    me = 0
    for axis, size in zip(axes, sizes):
        me = me * size + lax.axis_index(axis)

    def at(member):
        device = {}
        for axis, size in reversed(list(zip(axes, sizes))):
            device[axis] = member % size
            member = member // size
        return device

    barrier = pltpu.get_barrier_semaphore()

    @pl.loop(1, group)
    def _(step):
        pl.semaphore_signal(
            barrier,
            inc=1,
            device_id=at(lax.rem(me + step, group)),
            device_id_type=pl.DeviceIdType.MESH,
        )

    pl.semaphore_wait(barrier, group - 1)
    own = pltpu.make_async_copy(in_ref.at[me], out_ref.at[me], own_sem)
    own.start()

    def copy(to, slot):
        return pltpu.make_async_remote_copy(
            src_ref=in_ref.at[to],
            dst_ref=out_ref.at[slot],
            send_sem=send.at[to],
            recv_sem=recv.at[slot],
            device_id=at(to),
            device_id_type=pl.DeviceIdType.MESH,
        )

    @pl.loop(1, group)
    def _(step):
        copy(lax.rem(me + step, group), me).start()

    @pl.loop(1, group)
    def _(step):
        to = lax.rem(me + step, group)
        arrival = copy(to, to)
        arrival.wait_recv()
        arrival.wait_send()

    own.wait()


def exchange(blocks, axes, collective_id):
    group = blocks.shape[0]
    dma = pltpu.SemaphoreType.DMA
    return pl.pallas_call(
        functools.partial(exchange_kernel, axes),
        out_shape=jax.ShapeDtypeStruct(blocks.shape, blocks.dtype),
        in_specs=[pl.BlockSpec(memory_space=pltpu.VMEM)],
        out_specs=pl.BlockSpec(memory_space=pl.ANY),
        scratch_shapes=[dma((group,)), dma((group,)), dma],
        compiler_params=pltpu.CompilerParams(
            collective_id=collective_id, has_side_effects=True
        ),
        cost_estimate=pl.CostEstimate(flops=0, bytes_accessed=60_000_000, transcendentals=0),
    )(blocks)


def local(
    tokens,
    attn_gain,
    ffn_gain,
    w_attn,
    kv_pool,
    page_table,
    cache_len,
    routes,
    route_gain,
    w_gate_up,
    w_down,
):
    group = lax.axis_size("y") * lax.axis_size("zh") * lax.axis_size("zl")
    split = lax.axis_size("zl")
    part = lax.axis_index("zl")
    tok_dev, width = tokens.shape
    span = tok_dev * group
    length = cache_len[0]

    n_dp = lax.axis_size("dp")
    stripe = width // n_dp
    own_w = lax.dynamic_slice_in_dim(w_attn, lax.axis_index("dp") * stripe, stripe, 1)
    own_w = jnp.transpose(own_w, (0, 2, 1))
    sent_w = own_w[:3]
    normed = rms_scale(tokens, attn_gain)
    head_w, piece, arrived, out_w = spread(sent_w, normed, kv_pool, own_w[3])
    project_w = head_w.reshape(3 * HD, width)
    piece = piece.reshape(-1, width)

    slots = kv_pool.shape[0]
    page = kv_pool.shape[2]
    sub = page // split
    cached = arrived.reshape(group * slots * sub, 2 * HD)

    gate_up = lax.all_gather(w_gate_up, "y", axis=0, tiled=True)

    place_of = jnp.arange(piece.shape[0], dtype=jnp.int32)
    positions = length + (place_of // tok_dev * split + part) * tok_dev + place_of % tok_dev
    product = lax.dot_general(
        piece, project_w, (((1,), (1,)), ((), ())), preferred_element_type=jnp.float32
    )
    query = rotate(product[:, :HD], positions).astype(jnp.bfloat16)
    key_new = rotate(product[:, HD : 2 * HD], positions).astype(jnp.bfloat16)
    fresh = jnp.concatenate([key_new, product[:, 2 * HD :].astype(jnp.bfloat16)], axis=1)

    query = query.reshape(1, group // split, tok_dev, HD)
    query = jnp.broadcast_to(query, (split,) + query.shape[1:])
    query = lax.all_to_all(query, "zl", split_axis=0, concat_axis=0, tiled=True)
    query = jnp.transpose(query, (1, 0, 2, 3)).reshape(span, HD)

    table = page_table[0]
    slot_ids = jnp.arange(group * slots, dtype=jnp.int32)
    hits = table[None, :] == slot_ids[:, None]
    page_of = jnp.sum(
        jnp.where(hits, jnp.arange(table.shape[0], dtype=jnp.int32)[None, :], 0), axis=1
    )
    present = jnp.any(hits, axis=1)
    position = page_of[:, None] * page + part * sub + jnp.arange(sub, dtype=jnp.int32)[None, :]
    live = (present[:, None] & (position < length)).reshape(1, -1)
    bias = jnp.where(live, 0.0, very_low).astype(jnp.float32)

    packed = attend(query, cached, fresh, bias)
    packed, out_w, gate_up = lax.optimization_barrier((packed, out_w, gate_up))
    out_w = lax.all_gather(out_w.reshape(HEADS * HD, stripe), "dp", axis=0)
    landed_rows = exchange(packed.reshape(group, tok_dev, 2 * HD), GROUP, 1)
    landed_rows, w_down = lax.optimization_barrier((landed_rows, w_down))
    down = lax.all_gather(w_down, "y", axis=0, tiled=True)
    landed_rows = landed_rows.astype(jnp.float32).reshape(HEADS, split, tok_dev, 2 * HD)
    tops = landed_rows[..., HD]
    weight = jnp.exp(tops - jnp.max(tops, axis=1, keepdims=True))
    totals = jnp.sum(weight * (landed_rows[..., HD + 1] + landed_rows[..., HD + 2]), axis=1)
    numer = jnp.sum(weight[..., None] * landed_rows[..., :HD], axis=1)
    merged = numer / totals[..., None]
    merged = jnp.transpose(merged, (1, 0, 2)).reshape(tok_dev, HEADS * HD)
    attn = jnp.einsum(
        "tk,dkn->tdn", merged.astype(jnp.bfloat16), out_w, preferred_element_type=jnp.float32
    ).reshape(tok_dev, width)
    hidden = (tokens.astype(jnp.float32) + attn).astype(jnp.bfloat16)
    normed2 = rms_scale(hidden, ffn_gain)

    cap = max(2, tok_dev * TOP * 5 // (4 * EXPERTS))
    flat_expert = routes.reshape(-1)
    onehot = (flat_expert[:, None] == jnp.arange(EXPERTS, dtype=jnp.int32)[None, :]).astype(
        jnp.int32
    )
    rank = jnp.sum(jnp.cumsum(onehot, axis=0) * onehot, axis=1) - 1
    slot_id = flat_expert * cap + rank
    total_slots = EXPERTS * cap
    place = (slot_id[:, None] == jnp.arange(total_slots, dtype=jnp.int32)[None, :]).astype(
        jnp.float32
    )
    token_of = (
        jnp.arange(tok_dev * TOP, dtype=jnp.int32)[:, None] // TOP
        == jnp.arange(tok_dev, dtype=jnp.int32)[None, :]
    ).astype(jnp.float32)
    dispatch = jnp.dot(place.T, token_of, precision=lax.Precision.HIGHEST).astype(jnp.bfloat16)
    combine = jnp.dot(
        token_of.T, place * route_gain.reshape(-1)[:, None], precision=lax.Precision.HIGHEST
    )
    buffer = jnp.dot(dispatch, normed2, preferred_element_type=jnp.float32).astype(jnp.bfloat16)
    landed = exchange(
        buffer.reshape(EXPERTS, cap, width // HD, HD), EXPERT_AXES, 2
    ).reshape(total_slots, width)

    units = w_down.shape[1]
    both = jnp.einsum("rd,qdf->qrf", landed, gate_up, preferred_element_type=jnp.float32)
    activation = (jax.nn.silu(both[..., :units]) * both[..., units:]).astype(jnp.bfloat16)
    summed = jnp.einsum("qrf,qfd->rd", activation, down, preferred_element_type=jnp.float32)
    output_rows = exchange(
        summed.astype(jnp.bfloat16).reshape(EXPERTS, cap, width // HD, HD), EXPERT_AXES, 3
    ).reshape(total_slots, width)
    moe = jnp.dot(combine, output_rows.astype(jnp.float32), precision=lax.Precision.HIGHEST)
    return (hidden.astype(jnp.float32) + moe).astype(jnp.bfloat16)


def solution(mesh):
    n_dp, n_tensor = mesh.devices.shape
    inner = Mesh(
        mesh.devices.reshape(n_dp, n_tensor // 8, 2, 4), ("dp", "y", "zh", "zl")
    )
    everywhere = ("dp",) + GROUP
    placed = (
        P(everywhere, None),
        P(),
        P(),
        P(None, None, GROUP),
        P(everywhere, None, None, None),
        P("dp", None),
        P("dp"),
        P(everywhere, None),
        P(everywhere, None),
        P(everywhere, None, None),
        P(everywhere, None, None),
    )
    return jax.shard_map(
        local, mesh=inner, in_specs=placed, out_specs=P(everywhere, None), check_vma=False
    )
```

```python
import functools
import math

import jax
import jax.numpy as jnp
from jax import lax
from jax.experimental import pallas as pl
from jax.experimental.pallas import tpu as pltpu
from jax.sharding import Mesh, PartitionSpec as P

HEADS = 8
HD = 128
EXPERTS = 64
TOP = 4

rope_base = 50000.0
norm_eps = 1e-06
very_low = -1e30

GROUP = ("y", "zh", "zl")
EXPERT_AXES = ("dp", "zh", "zl")


def rms_scale(rows, gain):
    values = rows.astype(jnp.float32)
    power = jnp.mean(values * values, axis=-1, keepdims=True)
    return (values * lax.rsqrt(power + norm_eps) * gain).astype(jnp.bfloat16)


def rotate(values, positions):
    half = values.shape[-1] // 2
    freq = rope_base ** (-(jnp.arange(half, dtype=jnp.float32) * 2.0) / values.shape[-1])
    angle = positions.astype(jnp.float32)[:, None] * freq[None, :]
    cosine = jnp.cos(angle)
    sine = jnp.sin(angle)
    first = values[:, :half]
    second = values[:, half:]
    return jnp.concatenate([first * cosine - second * sine, second * cosine + first * sine], axis=1)


def attend_kernel(q_ref, kv_ref, new_ref, bias_ref, out_ref):
    q = q_ref[...]
    scale = 1.0 / math.sqrt(HD)
    old = kv_ref.shape[0]
    nt = (((1,), (1,)), ((), ()))
    s_old = lax.dot_general(q, kv_ref[:, :HD], nt, preferred_element_type=jnp.float32) * scale
    s_old = jnp.where(bias_ref[...] < 0.0, very_low, s_old)
    s_new = lax.dot_general(q, new_ref[:, :HD], nt, preferred_element_type=jnp.float32) * scale
    top = jnp.maximum(
        jnp.max(s_old, axis=1, keepdims=True), jnp.max(s_new, axis=1, keepdims=True)
    )
    top = top.astype(jnp.bfloat16).astype(jnp.float32)
    e_old = jnp.exp(s_old - top)
    e_new = jnp.exp(s_new - top)
    total = jnp.sum(e_old, axis=1, keepdims=True) + jnp.sum(e_new, axis=1, keepdims=True)
    mixed = jnp.dot(
        e_old.astype(jnp.bfloat16), kv_ref[:, HD:], preferred_element_type=jnp.float32
    ) + jnp.dot(e_new.astype(jnp.bfloat16), new_ref[:, HD:], preferred_element_type=jnp.float32)
    out_ref[:, :HD] = mixed.astype(jnp.bfloat16)
    coarse = total.astype(jnp.bfloat16).astype(jnp.float32)
    lane = lax.broadcasted_iota(jnp.int32, (q.shape[0], HD), 1)
    stats = jnp.where(lane == 0, top, jnp.where(lane == 1, coarse, total - coarse))
    out_ref[:, HD:] = stats.astype(jnp.bfloat16)


def attend(query, cached, fresh, bias):
    rows = query.shape[0]
    block = math.gcd(rows, 256)
    old, new = cached.shape[0], fresh.shape[0]
    return pl.pallas_call(
        attend_kernel,
        grid=(rows // block,),
        out_shape=jax.ShapeDtypeStruct((rows, 2 * HD), jnp.bfloat16),
        in_specs=[
            pl.BlockSpec((block, HD), lambda i: (i, 0)),
            pl.BlockSpec((old, 2 * HD), lambda i: (0, 0)),
            pl.BlockSpec((new, 2 * HD), lambda i: (0, 0)),
            pl.BlockSpec((1, old), lambda i: (0, 0)),
        ],
        out_specs=pl.BlockSpec((block, 2 * HD), lambda i: (i, 0)),
        cost_estimate=pl.CostEstimate(
            flops=4 * rows * (old + new) * HD,
            bytes_accessed=6 * (rows + old + new) * HD,
            transcendentals=rows * (old + new),
        ),
    )(query, cached, fresh, bias)


def spread_kernel(
    w_ref,
    n_ref,
    kv_ref,
    o_ref,
    w_out,
    n_out,
    kv_out,
    o_out,
    w_sem,
    dp_sem,
    n_sem,
    kv_send,
    kv_recv,
    o_send,
    o_recv,
    own_sem,
):
    n_y, n_zh, n_zl = lax.axis_size("y"), lax.axis_size("zh"), lax.axis_size("zl")
    y, zh, zl = lax.axis_index("y"), lax.axis_index("zh"), lax.axis_index("zl")
    group = n_y * n_zh * n_zl
    me = (y * n_zh + zh) * n_zl + zl
    slot = y * n_zh + zh
    over = lax.rem(zh + 1, n_zh)
    over_slot = y * n_zh + over
    sub = kv_ref.shape[2] // n_zl
    n_dp, dp = lax.axis_size("dp"), lax.axis_index("dp")
    stripe = w_ref.shape[2]

    def columns(which):
        return pl.ds(pl.multiple_of(which * stripe, stripe), stripe)

    def at(member):
        return {"y": member // (n_zh * n_zl), "zh": member // n_zl % n_zh, "zl": member % n_zl}

    def copy(src, dst, send, recv, device):
        return pltpu.make_async_remote_copy(
            src_ref=src,
            dst_ref=dst,
            send_sem=send,
            recv_sem=recv,
            device_id=device,
            device_id_type=pl.DeviceIdType.MESH,
        )

    barrier = pltpu.get_barrier_semaphore()

    @pl.loop(1, group)
    def _(step):
        pl.semaphore_signal(
            barrier,
            inc=1,
            device_id=at(lax.rem(me + step, group)),
            device_id_type=pl.DeviceIdType.MESH,
        )

    @pl.loop(1, n_dp)
    def _(step):
        pl.semaphore_signal(
            barrier,
            inc=1,
            device_id={"dp": lax.rem(dp + step, n_dp)},
            device_id_type=pl.DeviceIdType.MESH,
        )

    pl.semaphore_wait(barrier, group + n_dp - 2)

    def pages(member):
        rows = pl.ds(pl.multiple_of(member % n_zl * sub, sub), sub)
        return kv_ref.at[:, member // n_zl, rows, :]

    own = [
        pltpu.make_async_copy(w_ref, w_out.at[:, zl, :, columns(dp)], own_sem.at[0]),
        pltpu.make_async_copy(n_ref, n_out.at[slot], own_sem.at[1]),
        pltpu.make_async_copy(pages(me), kv_out.at[me], own_sem.at[2]),
        pltpu.make_async_copy(o_ref, o_out.at[me], own_sem.at[3]),
    ]
    across = copy(n_ref, n_out.at[slot], n_sem.at[0, 0], n_sem.at[1, slot], {"zh": over})
    across.start()
    near = []
    for step in (1, 3, 2):
        device = {"y": lax.rem(y + step, n_y)}
        near.append(
            copy(n_ref, n_out.at[slot], n_sem.at[0, step], n_sem.at[1, slot], device)
        )
        near[-1].start()
    heads = []
    for step in (1, 3, 2):
        device = {"zl": lax.rem(zl + step, n_zl)}
        heads.append(
            copy(
                w_ref,
                w_out.at[:, zl, :, columns(dp)],
                w_sem.at[0, step],
                w_sem.at[1, zl],
                device,
            )
        )
        heads[-1].start()
    for item in own:
        item.start()

    @pl.loop(1, group)
    def _(step):
        to = lax.rem(me + step, group)
        copy(pages(to), kv_out.at[me], kv_send.at[to], kv_recv.at[me], at(to)).start()
        copy(o_ref, o_out.at[me], o_send.at[to], o_recv.at[me], at(to)).start()

    copy(
        n_ref, n_out.at[over_slot], n_sem.at[0, 0], n_sem.at[1, over_slot], {"zh": over}
    ).wait_recv()
    for step in (1, 3, 2):
        device = {"y": lax.rem(y + step, n_y)}
        near.append(
            copy(
                n_out.at[over_slot],
                n_out.at[over_slot],
                n_sem.at[0, 4 + step],
                n_sem.at[1, over_slot],
                device,
            )
        )
        near[-1].start()

    own[0].wait()
    for step in (1, 3, 2):
        there = lax.rem(zl + step, n_zl)
        copy(
            w_ref,
            w_out.at[:, there, :, columns(dp)],
            w_sem.at[0, 0],
            w_sem.at[1, there],
            {"zl": there},
        ).wait_recv()

    def stripes(to, which):
        return copy(
            w_out.at[:, :, :, columns(which)],
            w_out.at[:, :, :, columns(which)],
            dp_sem.at[0, to],
            dp_sem.at[1, which],
            {"dp": to},
        )

    @pl.loop(1, n_dp)
    def _(step):
        stripes(lax.rem(dp + step, n_dp), dp).start()

    for step in (1, 3, 2):
        other = lax.rem(y + step, n_y)
        for half in range(2):
            there = other * n_zh + half
            copy(
                n_ref, n_out.at[there], n_sem.at[0, 0], n_sem.at[1, there], {"y": other}
            ).wait_recv()

    @pl.loop(1, group)
    def _(step):
        to = lax.rem(me + step, group)
        arrival = copy(pages(to), kv_out.at[to], kv_send.at[to], kv_recv.at[to], at(to))
        arrival.wait_recv()
        arrival.wait_send()
        arrival = copy(o_ref, o_out.at[to], o_send.at[to], o_recv.at[to], at(to))
        arrival.wait_recv()
        arrival.wait_send()

    @pl.loop(1, n_dp)
    def _(step):
        other = lax.rem(dp + step, n_dp)
        stripes(other, other).wait_recv()
        stripes(other, dp).wait_send()

    across.wait_send()
    for item in near + heads:
        item.wait_send()
    for item in own[1:]:
        item.wait()


def spread(sent_w, normed, kv_pool, sent_o):
    n_y, n_zh, n_zl = lax.axis_size("y"), lax.axis_size("zh"), lax.axis_size("zl")
    group = n_y * n_zh * n_zl
    slots, _, page, lanes = kv_pool.shape
    kinds, cols, stripe = sent_w.shape
    n_dp = lax.axis_size("dp")
    dma = pltpu.SemaphoreType.DMA
    return pl.pallas_call(
        spread_kernel,
        out_shape=(
            jax.ShapeDtypeStruct((kinds, n_zl, cols, n_dp * stripe), jnp.bfloat16),
            jax.ShapeDtypeStruct((n_y * n_zh,) + normed.shape, jnp.bfloat16),
            jax.ShapeDtypeStruct((group, slots, page // n_zl, lanes), jnp.bfloat16),
            jax.ShapeDtypeStruct((group,) + sent_o.shape, jnp.bfloat16),
        ),
        in_specs=[pl.BlockSpec(memory_space=pltpu.VMEM)] * 4,
        out_specs=(pl.BlockSpec(memory_space=pl.ANY),) * 4,
        scratch_shapes=[
            dma((2, n_zl)),
            dma((2, n_dp)),
            dma((2, n_y * n_zh)),
            dma((group,)),
            dma((group,)),
            dma((group,)),
            dma((group,)),
            dma((4,)),
        ],
        compiler_params=pltpu.CompilerParams(collective_id=0, has_side_effects=True),
        cost_estimate=pl.CostEstimate(
            flops=0, bytes_accessed=100_000_000, transcendentals=0
        ),
    )(sent_w, normed, kv_pool, sent_o)


def exchange_kernel(axes, in_ref, out_ref, send, recv, own_sem):
    sizes = [lax.axis_size(axis) for axis in axes]
    group = math.prod(sizes)
    me = 0
    for axis, size in zip(axes, sizes):
        me = me * size + lax.axis_index(axis)

    def at(member):
        device = {}
        for axis, size in reversed(list(zip(axes, sizes))):
            device[axis] = member % size
            member = member // size
        return device

    barrier = pltpu.get_barrier_semaphore()

    @pl.loop(1, group)
    def _(step):
        pl.semaphore_signal(
            barrier,
            inc=1,
            device_id=at(lax.rem(me + step, group)),
            device_id_type=pl.DeviceIdType.MESH,
        )

    pl.semaphore_wait(barrier, group - 1)
    own = pltpu.make_async_copy(in_ref.at[me], out_ref.at[me], own_sem)
    own.start()

    def copy(to, slot):
        return pltpu.make_async_remote_copy(
            src_ref=in_ref.at[to],
            dst_ref=out_ref.at[slot],
            send_sem=send.at[to],
            recv_sem=recv.at[slot],
            device_id=at(to),
            device_id_type=pl.DeviceIdType.MESH,
        )

    @pl.loop(1, group)
    def _(step):
        copy(lax.rem(me + step, group), me).start()

    @pl.loop(1, group)
    def _(step):
        to = lax.rem(me + step, group)
        arrival = copy(to, to)
        arrival.wait_recv()
        arrival.wait_send()

    own.wait()


def exchange(blocks, axes, collective_id):
    group = blocks.shape[0]
    dma = pltpu.SemaphoreType.DMA
    return pl.pallas_call(
        functools.partial(exchange_kernel, axes),
        out_shape=jax.ShapeDtypeStruct(blocks.shape, blocks.dtype),
        in_specs=[pl.BlockSpec(memory_space=pltpu.VMEM)],
        out_specs=pl.BlockSpec(memory_space=pl.ANY),
        scratch_shapes=[dma((group,)), dma((group,)), dma],
        compiler_params=pltpu.CompilerParams(
            collective_id=collective_id, has_side_effects=True
        ),
        cost_estimate=pl.CostEstimate(flops=0, bytes_accessed=60_000_000, transcendentals=0),
    )(blocks)


def local(
    tokens,
    attn_gain,
    ffn_gain,
    w_attn,
    kv_pool,
    page_table,
    cache_len,
    routes,
    route_gain,
    w_gate_up,
    w_down,
):
    group = lax.axis_size("y") * lax.axis_size("zh") * lax.axis_size("zl")
    split = lax.axis_size("zl")
    part = lax.axis_index("zl")
    tok_dev, width = tokens.shape
    span = tok_dev * group
    length = cache_len[0]

    n_dp = lax.axis_size("dp")
    stripe = width // n_dp
    own_w = lax.dynamic_slice_in_dim(w_attn, lax.axis_index("dp") * stripe, stripe, 1)
    own_w = jnp.transpose(own_w, (0, 2, 1))
    sent_w = own_w[:3]
    normed = rms_scale(tokens, attn_gain)
    head_w, piece, arrived, out_w = spread(sent_w, normed, kv_pool, own_w[3])
    project_w = head_w.reshape(3 * HD, width)
    piece = piece.reshape(-1, width)

    slots = kv_pool.shape[0]
    page = kv_pool.shape[2]
    sub = page // split
    cached = arrived.reshape(group * slots * sub, 2 * HD)

    gate_up = lax.all_gather(w_gate_up, "y", axis=0, tiled=True)

    place_of = jnp.arange(piece.shape[0], dtype=jnp.int32)
    positions = length + (place_of // tok_dev * split + part) * tok_dev + place_of % tok_dev
    product = lax.dot_general(
        piece, project_w, (((1,), (1,)), ((), ())), preferred_element_type=jnp.float32
    )
    query = rotate(product[:, :HD], positions).astype(jnp.bfloat16)
    key_new = rotate(product[:, HD : 2 * HD], positions).astype(jnp.bfloat16)
    fresh = jnp.concatenate([key_new, product[:, 2 * HD :].astype(jnp.bfloat16)], axis=1)

    query = query.reshape(1, group // split, tok_dev, HD)
    query = jnp.broadcast_to(query, (split,) + query.shape[1:])
    query = lax.all_to_all(query, "zl", split_axis=0, concat_axis=0, tiled=True)
    query = jnp.transpose(query, (1, 0, 2, 3)).reshape(span, HD)

    table = page_table[0]
    slot_ids = jnp.arange(group * slots, dtype=jnp.int32)
    hits = table[None, :] == slot_ids[:, None]
    page_of = jnp.sum(
        jnp.where(hits, jnp.arange(table.shape[0], dtype=jnp.int32)[None, :], 0), axis=1
    )
    present = jnp.any(hits, axis=1)
    position = page_of[:, None] * page + part * sub + jnp.arange(sub, dtype=jnp.int32)[None, :]
    live = (present[:, None] & (position < length)).reshape(1, -1)
    bias = jnp.where(live, 0.0, very_low).astype(jnp.float32)

    packed = attend(query, cached, fresh, bias)
    packed, out_w, gate_up = lax.optimization_barrier((packed, out_w, gate_up))
    out_w = lax.all_gather(out_w.reshape(HEADS * HD, stripe), "dp", axis=0)
    landed_rows = exchange(packed.reshape(group, tok_dev, 2 * HD), GROUP, 1)
    landed_rows, w_down = lax.optimization_barrier((landed_rows, w_down))
    down = lax.all_gather(w_down, "y", axis=0, tiled=True)
    landed_rows = landed_rows.astype(jnp.float32).reshape(HEADS, split, tok_dev, 2 * HD)
    tops = landed_rows[..., HD]
    weight = jnp.exp(tops - jnp.max(tops, axis=1, keepdims=True))
    totals = jnp.sum(weight * (landed_rows[..., HD + 1] + landed_rows[..., HD + 2]), axis=1)
    numer = jnp.sum(weight[..., None] * landed_rows[..., :HD], axis=1)
    merged = numer / totals[..., None]
    merged = jnp.transpose(merged, (1, 0, 2)).reshape(tok_dev, HEADS * HD)
    merged = merged.astype(jnp.bfloat16)
    attn = jnp.concatenate(
        [jnp.dot(merged, out_w[i], preferred_element_type=jnp.float32) for i in range(n_dp)],
        axis=1,
    )
    hidden = (tokens.astype(jnp.float32) + attn).astype(jnp.bfloat16)
    normed2 = rms_scale(hidden, ffn_gain)

    cap = max(2, tok_dev * TOP * 5 // (4 * EXPERTS))
    flat_expert = routes.reshape(-1)
    onehot = (flat_expert[:, None] == jnp.arange(EXPERTS, dtype=jnp.int32)[None, :]).astype(
        jnp.int32
    )
    rank = jnp.sum(jnp.cumsum(onehot, axis=0) * onehot, axis=1) - 1
    slot_id = flat_expert * cap + rank
    total_slots = EXPERTS * cap
    place = (slot_id[:, None] == jnp.arange(total_slots, dtype=jnp.int32)[None, :]).astype(
        jnp.float32
    )
    token_of = (
        jnp.arange(tok_dev * TOP, dtype=jnp.int32)[:, None] // TOP
        == jnp.arange(tok_dev, dtype=jnp.int32)[None, :]
    ).astype(jnp.float32)
    dispatch = jnp.dot(place.T, token_of, precision=lax.Precision.HIGHEST).astype(jnp.bfloat16)
    combine = jnp.dot(
        token_of.T, place * route_gain.reshape(-1)[:, None], precision=lax.Precision.HIGHEST
    )
    buffer = jnp.dot(dispatch, normed2, preferred_element_type=jnp.float32).astype(jnp.bfloat16)
    landed = exchange(
        buffer.reshape(EXPERTS, cap, width // HD, HD), EXPERT_AXES, 2
    ).reshape(total_slots, width)

    units = w_down.shape[1]
    both = jnp.einsum("rd,qdf->qrf", landed, gate_up, preferred_element_type=jnp.float32)
    activation = (jax.nn.silu(both[..., :units]) * both[..., units:]).astype(jnp.bfloat16)
    summed = jnp.einsum("qrf,qfd->rd", activation, down, preferred_element_type=jnp.float32)
    output_rows = exchange(
        summed.astype(jnp.bfloat16).reshape(EXPERTS, cap, width // HD, HD), EXPERT_AXES, 3
    ).reshape(total_slots, width)
    moe = jnp.dot(combine, output_rows.astype(jnp.float32), precision=lax.Precision.HIGHEST)
    return (hidden.astype(jnp.float32) + moe).astype(jnp.bfloat16)


def solution(mesh):
    n_dp, n_tensor = mesh.devices.shape
    inner = Mesh(
        mesh.devices.reshape(n_dp, n_tensor // 8, 2, 4), ("dp", "y", "zh", "zl")
    )
    everywhere = ("dp",) + GROUP
    placed = (
        P(everywhere, None),
        P(),
        P(),
        P(None, None, GROUP),
        P(everywhere, None, None, None),
        P("dp", None),
        P("dp"),
        P(everywhere, None),
        P(everywhere, None),
        P(everywhere, None, None),
        P(everywhere, None, None),
    )
    return jax.shard_map(
        local, mesh=inner, in_specs=placed, out_specs=P(everywhere, None), check_vma=False
    )
```
